32 devices in a mesh: tm: 16 (over z, y, x), replay: 2 (over core).
Axes of the slice: x: 2, y: 2, z: 4, core: 2. Of those that a mesh axis runs over, the one named last changes fastest.
Arguments:
- obs_store: float32 [2, 1024, 64], P('replay', 'tm'), may hold values from -240 to 240
- observed: int32 [2048], P(('tm', 'replay')), may hold values 0 or 1
- transition: float32 [128, 128], replicated, may hold values from -1 to 1, as said below
- obs_map: float32 [64, 128], replicated, may hold values from -0.5 to 0.5
- gain_weights: float32 [64], replicated, may hold values from 0.00048828125 to 0.009765625
- init_mean: float32 [128], replicated, may hold values from -6 to 6
- smoothed_cov: float32 [128, 128], replicated, may hold values from -0.01 to 0.8, as said below
Outputs:
- smoothed: float32 [2048, 128], P(('tm', 'replay'))
- new_transition: float32 [128, 128], replicated
The draws below stay inside these ranges and needn't reach their ends.
Inputs may be any that keep to these rules, and one draw needn't show every extreme that they name: `transition`: its spectral norm is below 1. `smoothed_cov`: symmetric positive definite.
All inputs are finite; a program needn't handle non-finite values. No bound on the sum of `observed` on one device may be relied on, other than what follows from the above.
Results may differ from the reference program's by a relative error of at most 0.0003.
Values sent between devices are 32-bit elements; how exact they have to be, the bound alone decides.
A program may use at most 128 MiB of HBM per device.

```python
import math
import jax
import jax.numpy as jnp
from jax import lax

S = 128
M = 64
STEPS_DEV = 64
TIME = 2048
N_TM = 16


def draw_transition(key, part):
    key_rate, key_angle = jax.random.split(key)
    pair_count = S // 2
    rates = jnp.exp(jax.random.uniform(key_rate, (pair_count,), jnp.float32, math.log(0.2 / TIME), math.log(1.0 / 32.0)))
    angles = jax.random.uniform(key_angle, (pair_count,), jnp.float32, -math.pi, math.pi)
    block_ids = jnp.arange(S) // 2
    parity = jnp.arange(S) % 2
    decay_rows = jnp.exp(-rates)[block_ids]
    cosine = jnp.cos(angles)[block_ids]
    sine_rows = jnp.sin(angles)[block_ids]
    same_block = block_ids[:, None] == block_ids[None, :]
    on_diagonal = parity[:, None] == parity[None, :]
    above_diag = parity[:, None] < parity[None, :]
    values = jnp.where(on_diagonal, cosine[:, None], jnp.where(above_diag, -sine_rows[:, None], sine_rows[:, None]))
    return jnp.where(same_block, values * decay_rows[:, None], 0.0).astype(jnp.float32)


def draw_smoothed_cov(key, part):
    key_scale, key_mix = jax.random.split(key)
    scales = jnp.exp(jax.random.uniform(key_scale, (S,), jnp.float32, math.log(0.05), math.log(0.5)))
    noise_draw = jax.random.uniform(key_mix, (S, S), jnp.float32, -1.0, 1.0)
    symmetric = 0.5 * (noise_draw + noise_draw.T)
    identity = jnp.eye(S, dtype=jnp.float32)
    shape_mat = identity + 0.9 / S * symmetric * (1.0 - identity)
    root_scale = jnp.sqrt(scales)
    return (root_scale[:, None] * shape_mat * root_scale[None, :]).astype(jnp.float32)


def place_ends(result, key, low, high):
    place = [jax.random.randint(jax.random.fold_in(key, axis), (), 0, length) for axis, length in enumerate(result.shape)]
    longest = result.shape.index(max(result.shape))
    beside = place[:longest] + [(place[longest] + 1) % result.shape[longest]] + place[longest + 1:]
    return result.at[tuple(place)].set(low).at[tuple(beside)].set(high)


def level_of(rng, extent, cuts, least, largest):
    gain, own = 1.0, jax.random.fold_in(rng, 6)
    for dim, parts in cuts:
        heights = jnp.exp(jax.random.uniform(jax.random.fold_in(own, dim), (parts,), jnp.float32, least / len(cuts), largest / len(cuts)))
        gain = gain * jnp.repeat(heights, extent[dim] // parts).reshape([-1 if axis == dim else 1 for axis in range(len(extent))])
    return gain


def gaussian(rng, shape, scale, reach, shards=(), held_as=jnp.bfloat16):
    loudness = level_of(rng, shape, shards, -0.22, 0.18) if shards else 1.0
    values = jax.random.normal(rng, shape, jnp.float32) * scale * loudness
    return jnp.minimum(jnp.maximum(values, -reach), reach).astype(held_as)


def setup_inputs(seed: int = 0) -> dict:
    key_list = jax.random.split(jax.random.key(seed), 8)
    return {
        "obs_store": gaussian(key_list[0], (2, TIME // 2, M), 40.0, 240.0, ((0, 2), (1, 16)), jnp.float32),
        "observed": place_ends((jax.random.randint(key_list[1], (TIME,), 0, 4) < 3).astype(jnp.int32), jax.random.fold_in(key_list[1], 1), 0, 1),
        "transition": draw_transition(jax.random.fold_in(key_list[7], 71), 0),
        "obs_map": gaussian(key_list[3], (M, S), S ** -0.5, 0.5, (), jnp.float32),
        "gain_weights": jnp.clip(jnp.exp(jax.random.uniform(key_list[4], (M,), jnp.float32, math.log(0.00048828125), math.log(0.009765625))), 0.00048828125, 0.009765625),
        "init_mean": gaussian(key_list[5], (S,), 1.0, 6.0, (), jnp.float32),
        "smoothed_cov": draw_smoothed_cov(jax.random.fold_in(key_list[7], 71), 0),
    }


def model_mats(transition, obs_map, gain_weights):
    precise = lax.Precision.HIGHEST
    gain_mat = obs_map.T * gain_weights[None, :]
    keep_mat = jnp.eye(transition.shape[0], dtype=jnp.float32) - jnp.dot(gain_mat, obs_map, precision=precise)
    corrected = jnp.dot(keep_mat, transition, precision=precise)
    back_gain = jnp.dot(keep_mat, transition.T, precision=precise)
    return (gain_mat, corrected, back_gain)

def solve_rows(cross_sum, square):
    factor = jnp.linalg.cholesky(square)
    half_solve = lax.linalg.triangular_solve(factor, cross_sum.T, left_side=True, lower=True)
    full_solve = lax.linalg.triangular_solve(factor, half_solve, left_side=True, lower=True, transpose_a=True)
    return full_solve.T

def reference(obs_store, observed, transition, obs_map, gain_weights, init_mean, smoothed_cov):
    precise = lax.Precision.HIGHEST
    gain_mat, corrected, back_gain = model_mats(transition, obs_map, gain_weights)
    series = obs_store.reshape(2, N_TM, STEPS_DEV, M).transpose(1, 2, 0, 3).reshape(TIME, M)
    flag_vals = observed.astype(jnp.float32)
    pushes = jnp.dot(series, gain_mat.T, precision=precise) * flag_vals[:, None]

    def filter_step(carried, inputs):
        flag_now, push_now = inputs
        matrix = jnp.where(flag_now > 0, corrected, transition)
        carried = jnp.dot(matrix, carried, precision=precise) + push_now
        return (carried, carried)
    final_state, filtered = lax.scan(filter_step, init_mean, (observed, pushes))
    back_mix = jnp.dot(back_gain, transition, precision=precise)
    blended = filtered - jnp.dot(filtered, back_mix.T, precision=precise)

    def smooth_step(carried, blend_now):
        carried = jnp.dot(back_gain, carried, precision=precise) + blend_now
        return (carried, carried)
    last_state, earlier = lax.scan(smooth_step, final_state, blended[:-1], reverse=True)
    smoothed = jnp.concatenate([earlier, filtered[-1:]], 0)
    previous = smoothed[:-1]
    current = smoothed[1:]
    pair_count = jnp.float32(TIME - 1)
    cross_sum = jnp.dot(current.T, previous, precision=precise) + pair_count * jnp.dot(smoothed_cov, back_gain.T, precision=precise)
    square_sum = jnp.dot(previous.T, previous, precision=precise) + pair_count * smoothed_cov
    return (smoothed, solve_rows(cross_sum, square_sum))
```

```python
import functools

import jax
import jax.numpy as jnp
from jax import lax
from jax.experimental import pallas as pl
from jax.experimental.pallas import tpu as pltpu
from jax.sharding import PartitionSpec as P

MESH = pl.DeviceIdType.MESH
F32 = jnp.float32


def mm(a, b):
    return jnp.dot(a, b, precision=lax.Precision.HIGHEST, preferred_element_type=F32)


def halves(a):
    high = a.astype(jnp.bfloat16)
    return high, (a - high.astype(F32)).astype(jnp.bfloat16)


def mm_apply(a, b):
    rows = a.shape[0]
    a_high, a_low = halves(a)
    b_high, b_low = halves(b)
    both = jnp.dot(jnp.concatenate([a_high, a_low], 0), b_high, preferred_element_type=F32)
    return both[:rows] + both[rows:] + jnp.dot(a_high, b_low, preferred_element_type=F32)


def apply_row(row, mat):
    return mm_apply(jnp.concatenate([row, row], 0), mat)[:8]


def mm_first(a, b):
    return lax.dot_general(
        a, b, (((0,), (0,)), ((), ())), precision=lax.Precision.HIGHEST, preferred_element_type=F32
    )


def eye(n):
    rows = lax.broadcasted_iota(jnp.int32, (n, n), 0)
    return rows == lax.broadcasted_iota(jnp.int32, (n, n), 1)


def column(row, n):
    return jnp.sum(jnp.where(eye(n), jnp.broadcast_to(row, (n, n)), 0.0), axis=1, keepdims=True)


def flip(place, bit):
    return place + bit * (1 - 2 * lax.rem(place // bit, 2))


def em_kernel(
    levels, obs_ref, flag_smem, flag_ref, trans_ref, map_ref, gain_ref, init_ref, cov_ref,
    smooth_ref, sums_ref,
    got_obs, table, push, flags, pad, send_map, got_map, send_vec, got_vec, sums, got_sums,
    held_tree, held_powers, send_sem, recv_sem,
):
    steps = push.shape[0]
    width = trans_ref.shape[0]
    chunks = steps // 4
    tm = lax.axis_index("tm")
    core = lax.axis_index("replay")
    place = tm * 2 + core
    last = 2**levels - 1

    def bit(k):
        return lax.rem(place // 2**k, 2)

    def target(mask):
        other = tm
        for k in range(1, levels):
            if mask >> k & 1:
                other = flip(other, 2 ** (k - 1))
        return (other, 1 - core if mask & 1 else core)

    stages = [(low, min(2, levels - low)) for low in range(0, levels, 2)]
    masks = sorted(
        {2**k for k in range(levels)} | {x << low for low, bits in stages for x in range(1, 2**bits)}
    )
    barrier = pltpu.get_barrier_semaphore()
    for mask in masks:
        pl.semaphore_signal(barrier, inc=1, device_id=target(mask), device_id_type=MESH)
    pl.semaphore_wait(barrier, len(masks))

    used = [0]

    def send(src, dst, mask):
        slot = used[0]
        used[0] += 1
        copy = pltpu.make_async_remote_copy(
            src_ref=src, dst_ref=dst, send_sem=send_sem.at[slot], recv_sem=recv_sem.at[slot],
            device_id=target(mask), device_id_type=MESH,
        )
        copy.start()
        return copy

    half = steps // 2
    away = pl.multiple_of((1 - core) * half, 8)
    near = pl.multiple_of(core * half, 8)
    obs_copy = send(obs_ref.at[0, pl.ds(away, half), :], got_obs, 1)

    trans = trans_ref[...]
    trans_t = trans.T
    scaled_map = map_ref[...] * column(gain_ref[...], gain_ref.shape[1])
    keep = jnp.where(eye(width), 1.0, 0.0) - mm_first(scaled_map, map_ref[...])
    corr_t = mm(trans_t, keep)
    back_t = mm(trans, keep)
    ones = [trans_t, corr_t]
    both = jnp.concatenate(ones, 1)
    twos = mm(jnp.concatenate(ones, 0), both)
    pairs = [twos[a * width:(a + 1) * width, b * width:(b + 1) * width] for a in range(2) for b in range(2)]
    wide = jnp.concatenate(pairs, 1)
    for a in range(4):
        fours = mm(pairs[a], wide)
        for b in range(4):
            table[a * 4 + b] = fours[:, b * width:(b + 1) * width]

    flags[...] = jnp.broadcast_to(column(flag_ref[...].astype(F32), steps), flags.shape)
    obs_copy.wait_recv()
    own_push = mm_apply(obs_ref[0, pl.ds(near, half), :], scaled_map)
    got_push = mm_apply(got_obs[...], scaled_map)
    push[pl.ds(0, half, stride=2), :] = jnp.where(core == 0, own_push, got_push)
    push[pl.ds(1, half, stride=2), :] = jnp.where(core == 0, got_push, own_push)

    step_flags = [flags[pl.ds(j, chunks, stride=4), :] for j in range(4)]
    step_push = [push[pl.ds(j, chunks, stride=4), :] * step_flags[j] for j in range(4)]

    def advance(state, j, times=mm):
        moved = times(state, both)
        return jnp.where(step_flags[j] > 0, moved[:, width:], moved[:, :width]) + step_push[j]

    state = step_push[0]
    for j in range(1, 4):
        state = advance(state, j, mm_apply)

    def quad(q):
        f = [flag_smem[4 * q + j] for j in range(4)]
        return table[f[0] * 8 + f[1] * 4 + f[2] * 2 + f[3]]

    def spread(row):
        return jnp.broadcast_to(row, (8, width))

    def compose(early, late):
        moved = mm(jnp.concatenate(early, 0), late[0])
        return (moved[:width], moved[width:] + late[1])

    placed = [0]

    def keep_node(mat, vec):
        at = placed[0]
        placed[0] += 1
        held_tree[at, :width] = mat
        held_tree[at, width:] = vec
        return at

    def node(at):
        return (held_tree[at, :width], held_tree[at, width:])

    tree = [[keep_node(quad(q), spread(state[q:q + 1])) for q in range(chunks)]]
    while len(tree[-1]) > 1:
        ids = tree[-1]
        tree.append(
            [keep_node(*compose(node(ids[i]), node(ids[i + 1]))) for i in range(0, len(ids), 2)]
        )
    total = node(tree[-1][0])

    held_powers[0] = back_t
    powers = {1: 0}

    def power(n):
        if n not in powers:
            low = n // 2 if n & (n - 1) == 0 else n & -n
            value = mm(power(low), power(n - low))
            powers[n] = len(powers)
            held_powers[powers[n]] = value
        return held_powers[powers[n]]

    ahead = [[1, 2, 3, 4], [8, 12, 16], [32, 48, 64], [128, 192, 256], [512, 768]]
    mix_t = mm(trans_t, back_t)
    copies = []
    before = None
    for k in range(levels):
        send_map[k, :width] = total[0]
        send_map[k, width:] = total[1]
        copies.append(send(send_map.at[k], got_map.at[k], 2**k))
        for n in ahead[k] if k < len(ahead) else []:
            power(n)
        if k == 1:
            before = (
                jnp.where(bit(0) == 1, got_map[0, :width], jnp.where(eye(width), 1.0, 0.0)),
                jnp.where(bit(0) == 1, got_map[0, width:], 0.0),
            )
        elif k > 1:
            longer = compose((got_map[k - 1, :width], got_map[k - 1, width:]), before)
            before = tuple(jnp.where(bit(k - 1) == 1, a, b) for a, b in zip(longer, before))
        copies[-1].wait_recv()
        if k < levels - 1:
            mine_late = bit(k) == 1
            got = (got_map[k, :width], got_map[k, width:])
            early = tuple(jnp.where(mine_late, a, b) for a, b in zip(got, total))
            late = tuple(jnp.where(mine_late, a, b) for a, b in zip(total, got))
            total = compose(early, late)
    begin = spread(init_ref[...])
    top = levels - 1
    begin = jnp.where(bit(top) == 1, mm(begin, got_map[top, :width]) + got_map[top, width:], begin)
    begin = mm(begin, before[0]) + before[1]

    heads = [begin]
    for ids in reversed(tree[:-1]):
        after = []
        for i, head in enumerate(heads):
            mat, vec = node(ids[2 * i])
            after.append(apply_row(head, mat) + vec)
        heads = [x for pair in zip(heads, after) for x in pair]
    lanes = lax.broadcasted_iota(jnp.int32, (8, width), 0)
    tiles = []
    for q in range(0, chunks, 8):
        tile = heads[q]
        for i in range(1, 8):
            tile = jnp.where(lanes == i, heads[q + i], tile)
        tiles.append(tile)
    state = jnp.concatenate(tiles, 0)
    for j in range(4):
        state = advance(state, j, mm_apply)
        push[pl.ds(j, chunks, stride=4), :] = state
    filtered = push[...]

    row_ids = lax.broadcasted_iota(jnp.int32, (steps, width), 0)
    final = jnp.logical_and(row_ids == steps - 1, place == last)
    blended = jnp.where(final, filtered, filtered - mm(filtered, mix_t))

    pad[steps:, :] = jnp.zeros((steps, width), F32)

    def suffixes(rows):
        stride = 1
        while stride < steps:
            pad[:steps, :] = rows
            moved = jnp.concatenate([pad[n * stride:n * stride + steps, :] for n in (1, 2, 3)], 1)
            rows = rows + mm_apply(moved, jnp.concatenate([power(n * stride) for n in (1, 2, 3)], 0))
            stride *= 4
        return rows

    partial = suffixes(blended)
    whole = spread(partial[:1])
    tails = []
    for at, (low, bits) in enumerate(stages):
        size = 2**bits
        mine = lax.rem(place // 2**low, size)
        send_vec[at] = whole
        sent = [
            send(send_vec.at[at], got_vec.at[at, x - 1], x << low) for x in range(1, size)
        ]
        copies += sent
        jumps = [power(n * steps * 2**low) for n in range(1, size)]
        onward = jnp.where(eye(width), 1.0, 0.0)
        for n in range(1, size):
            onward = jnp.where(mine == size - 1 - n, jumps[n - 1], onward)
        for copy in sent:
            copy.wait_recv()
        values = []
        for q in range(size):
            value = whole
            for x in range(1, size):
                other = mine
                for k in range(bits):
                    if x >> k & 1:
                        other = flip(other, 2**k)
                value = jnp.where(other == q, got_vec[at, x - 1], value)
            values.append(value)
        whole = values[0]
        for q in range(1, size):
            whole = whole + apply_row(values[q], jumps[q - 1])
        tail = jnp.zeros((8, width), F32)
        for q in reversed(range(1, size)):
            if q == size - 1:
                longer = values[q]
            else:
                longer = values[q] + apply_row(tail, jumps[0])
            tail = jnp.where(mine < q, longer, tail)
        tails.append((tail, onward))
    arriving = tails[-1][0]
    for tail, onward in reversed(tails[:-1]):
        arriving = tail + apply_row(arriving, onward)
    entry = jnp.where(row_ids == steps - 1, mm(arriving, back_t)[:1], 0.0)
    smoothed = partial + suffixes(entry)
    smooth_ref[...] = smoothed

    pad[:steps, :] = smoothed
    pad[steps:steps + 8, :] = arriving
    following = pad[1:steps + 1, :]
    counted = jnp.where(final, 0.0, smoothed)
    moments = mm_apply(counted.T, jnp.concatenate([smoothed, following], 1))
    sums[0] = moments[:, :width]
    sums[1] = moments[:, width:]
    copies.append(send(sums.at[1 - core], got_sums.at[0], 1))
    pair_count = F32(steps * (last + 1) - 1)
    lag_t = pair_count * lax.dot_general(
        back_t, cov_ref[...], (((0,), (1,)), ((), ())),
        precision=lax.Precision.HIGHEST, preferred_element_type=F32,
    )
    copies[-1].wait_recv()
    held = jnp.where(core == 0, moments[:, :width], moments[:, width:]) + got_sums[0]
    mid = width // 2
    parts = [held[:mid], held[mid:]]
    order = list(range(1, levels))
    turned = order[len(order) // 2:] + order[:len(order) // 2]
    for at, pair in enumerate(zip(order, turned), 1):
        sent = []
        for i, k in enumerate(pair):
            rows = pl.ds(i * mid, mid)
            sums[1 + at, rows, :] = parts[i]
            sent.append(send(sums.at[1 + at, rows, :], got_sums.at[at, rows, :], 2**k))
        copies += sent
        for i in range(2):
            sent[i].wait_recv()
            parts[i] = parts[i] + got_sums[at, i * mid:(i + 1) * mid, :]
    held = jnp.concatenate(parts, 0)
    sums[1 + levels] = held
    copies.append(send(sums.at[1 + levels], got_sums.at[levels], 1))
    copies[-1].wait_recv()
    other = got_sums[levels]
    sums_ref[:, :width] = jnp.where(core == 0, held, other) + pair_count * cov_ref[...]
    sums_ref[:, width:] = jnp.where(core == 0, other, held) + lag_t
    obs_copy.wait_send()
    for copy in copies:
        copy.wait_send()


def product(x, y):
    return [
        [sum((x[i][k] * y[k][j] for k in range(1, len(y))), x[i][0] * y[0][j]) for j in range(len(y[0]))]
        for i in range(len(x))
    ]


def small_inverse(d):
    n = len(d)
    if n == 1:
        return [[1.0 / d[0][0]]]
    if n == 2:
        det = 1.0 / (d[0][0] * d[1][1] - d[0][1] * d[0][1])
        off = -d[0][1] * det
        return [[d[1][1] * det, off], [off, d[0][0] * det]]
    h = n // 2
    head = small_inverse([r[:h] for r in d[:h]])
    side = [r[h:] for r in d[:h]]
    spread = product(head, side)
    fill = product([list(x) for x in zip(*side)], spread)
    rest = small_inverse([[d[h + i][h + j] - fill[i][j] for j in range(h)] for i in range(h)])
    back = product(spread, rest)
    fill = product(back, [list(x) for x in zip(*spread)])
    top = [[head[i][j] + fill[i][j] for j in range(h)] + [-x for x in back[i]] for i in range(h)]
    return top + [[-back[j][i] for j in range(h)] + rest[i] for i in range(h)]


def combine(rows, weights):
    total = rows[0] * weights[0]
    for row, weight in zip(rows[1:], weights[1:]):
        total = total + row * weight
    return total


def solve_kernel(sums_ref, smooth_ref, out_ref, smooth_out_ref):
    smooth_out_ref[...] = smooth_ref[...]
    width = out_ref.shape[0]
    groups = width // 8
    per = 4
    full = (8, width)
    left = [sums_ref[8 * g:8 * g + 8, :width] for g in range(groups)]
    right = [sums_ref[8 * g:8 * g + 8, width:] for g in range(groups)]
    lane = lax.broadcasted_iota(jnp.int32, (1, width), 1)
    sub = lax.broadcasted_iota(jnp.int32, full, 0)

    def spread_row(tile, i):
        return jnp.broadcast_to(tile[i:i + 1, :], full)

    for at in range(0, groups, per):
        panel = range(at, at + per)
        for pivot in panel:
            cols = {
                g: [jnp.broadcast_to(left[g][:, k:k + 1], full) for k in range(8 * pivot, 8 * pivot + 8)]
                for g in panel
            }
            inverse = small_inverse(
                [[spread_row(cols[pivot][max(i, j)], min(i, j)) for j in range(8)] for i in range(8)]
            )
            for side in (left, right):
                rows = [spread_row(side[pivot], j) for j in range(8)]
                solved = [combine(rows, inverse[i]) for i in range(8)]
                for g in panel:
                    if g == pivot:
                        tile = solved[0]
                        for j in range(1, 8):
                            tile = jnp.where(sub == j, solved[j], tile)
                        side[g] = tile
                    else:
                        side[g] = side[g] - combine(cols[g], solved)
        mask = jnp.logical_and(lane >= 8 * at, lane < 8 * (at + per))
        order = [g % groups for g in range(at + per, at + groups)]
        rows = [jnp.concatenate([left[g], right[g]], 1) for g in panel]
        before, after = 8 * at, 8 * (groups - at - per)
        if before:
            rows = [jnp.zeros((before, 2 * width), F32)] + rows
        if after:
            rows = rows + [jnp.zeros((after, 2 * width), F32)]
        change = mm(
            jnp.concatenate([jnp.where(mask, left[g], 0.0) for g in order], 0), jnp.concatenate(rows, 0)
        )
        for i, g in enumerate(order):
            left[g] = left[g] - change[8 * i:8 * i + 8, :width]
            right[g] = right[g] - change[8 * i:8 * i + 8, width:]
    out_ref[...] = jnp.concatenate(right, 0).T


def local(levels, obs_store, observed, transition, obs_map, gain_weights, init_mean, smoothed_cov):
    steps = observed.shape[0]
    width = transition.shape[0]
    vmem = pl.BlockSpec(memory_space=pltpu.VMEM)
    smem = pl.BlockSpec(memory_space=pltpu.SMEM)
    copies = 1 + levels + 3 * (levels + 1) // 2 + 2 * levels + 2
    smoothed, sums = pl.pallas_call(
        functools.partial(em_kernel, levels),
        out_shape=(
            jax.ShapeDtypeStruct((steps, width), F32),
            jax.ShapeDtypeStruct((width, 2 * width), F32),
        ),
        in_specs=[vmem, smem, vmem, vmem, vmem, vmem, vmem, vmem],
        out_specs=(vmem, vmem),
        scratch_shapes=[
            pltpu.VMEM((steps // 2, obs_map.shape[0]), F32),
            pltpu.VMEM((16, width, width), F32),
            pltpu.VMEM((steps, width), F32),
            pltpu.VMEM((steps, width), F32),
            pltpu.VMEM((2 * steps, width), F32),
            pltpu.VMEM((levels, width + 8, width), F32),
            pltpu.VMEM((levels, width + 8, width), F32),
            pltpu.VMEM((levels, 8, width), F32),
            pltpu.VMEM((levels, 3, 8, width), F32),
            pltpu.VMEM((levels + 2, width, width), F32),
            pltpu.VMEM((levels + 1, width, width), F32),
            pltpu.VMEM((steps // 2 - 1, width + 8, width), F32),
            pltpu.VMEM((24, width, width), F32),
            pltpu.SemaphoreType.DMA((copies,)),
            pltpu.SemaphoreType.DMA((copies,)),
        ],
        compiler_params=pltpu.CompilerParams(collective_id=0, has_side_effects=True),
    )(
        obs_store, observed, observed.reshape(1, -1), transition, obs_map,
        gain_weights.reshape(1, -1), init_mean.reshape(1, -1), smoothed_cov,
    )
    new_transition, smoothed = pl.pallas_call(
        solve_kernel,
        out_shape=(
            jax.ShapeDtypeStruct((width, width), F32),
            jax.ShapeDtypeStruct((steps, width), F32),
        ),
        in_specs=[vmem, vmem],
        out_specs=(vmem, vmem),
    )(sums, smoothed)
    return (smoothed, new_transition)


def solution(mesh):
    levels = (mesh.shape["tm"] * mesh.shape["replay"]).bit_length() - 1
    return jax.shard_map(
        functools.partial(local, levels),
        mesh=mesh,
        in_specs=(P("replay", "tm", None), P(("tm", "replay")), P(), P(), P(), P(), P()),
        out_specs=(P(("tm", "replay"), None), P()),
        check_vma=False,
    )
```

```python
import functools

import jax
import jax.numpy as jnp
from jax import lax
from jax.experimental import pallas as pl
from jax.experimental.pallas import tpu as pltpu
from jax.sharding import PartitionSpec as P

MESH = pl.DeviceIdType.MESH
F32 = jnp.float32


def mm(a, b):
    return jnp.dot(a, b, precision=lax.Precision.HIGHEST, preferred_element_type=F32)


def halves(a):
    high = a.astype(jnp.bfloat16)
    return high, (a - high.astype(F32)).astype(jnp.bfloat16)


def mm_apply(a, b):
    rows = a.shape[0]
    a_high, a_low = halves(a)
    b_high, b_low = halves(b)
    both = jnp.dot(jnp.concatenate([a_high, a_low], 0), b_high, preferred_element_type=F32)
    return both[:rows] + both[rows:] + jnp.dot(a_high, b_low, preferred_element_type=F32)


def mm_halves(a, b_halves):
    rows = a.shape[0]
    a_high, a_low = halves(a)
    both = jnp.dot(jnp.concatenate([a_high, a_low], 0), b_halves[0], preferred_element_type=F32)
    return both[:rows] + both[rows:] + jnp.dot(a_high, b_halves[1], preferred_element_type=F32)


def apply_row(row, mat):
    return mm_apply(jnp.concatenate([row, row], 0), mat)[:8]


def mm_first(a, b):
    return lax.dot_general(
        a, b, (((0,), (0,)), ((), ())), precision=lax.Precision.HIGHEST, preferred_element_type=F32
    )


def eye(n):
    rows = lax.broadcasted_iota(jnp.int32, (n, n), 0)
    return rows == lax.broadcasted_iota(jnp.int32, (n, n), 1)


def column(row, n):
    return jnp.sum(jnp.where(eye(n), jnp.broadcast_to(row, (n, n)), 0.0), axis=1, keepdims=True)


def flip(place, bit):
    return place + bit * (1 - 2 * lax.rem(place // bit, 2))


def em_kernel(
    levels, obs_ref, flag_smem, flag_ref, trans_ref, map_ref, gain_ref, init_ref, cov_ref,
    smooth_ref, sums_ref,
    got_obs, table, push, flags, pad, own_map, core_map, chip_maps, got_start, next_start, got_tails,
    moment, got_moment, line_moment, full_moment, held_tree, held_powers, send_sem, recv_sem,
):
    steps = push.shape[0]
    width = trans_ref.shape[0]
    chunks = steps // 4
    tm = lax.axis_index("tm")
    core = lax.axis_index("replay")
    place = tm * 2 + core
    count = 2**levels
    last = count - 1
    near_bits = 3
    mates = 2**near_bits
    lines = count // mates
    mine = lax.rem(place, mates)
    line = place // mates

    def at_place(other):
        return (other // 2, lax.rem(other, 2))

    def mate(mask):
        other = place
        for k in range(near_bits):
            if mask >> k & 1:
                other = flip(other, 2**k)
        return other

    barrier = pltpu.get_barrier_semaphore()
    for step in range(1, count):
        pl.semaphore_signal(
            barrier, inc=1, device_id=at_place(lax.rem(place + step, count)), device_id_type=MESH
        )

    used = [0]

    def remote(src, dst, other):
        slot = used[0]
        used[0] += 1
        return pltpu.make_async_remote_copy(
            src_ref=src, dst_ref=dst, send_sem=send_sem.at[slot], recv_sem=recv_sem.at[slot],
            device_id=at_place(other), device_id_type=MESH,
        )

    def send(src, dst, other):
        copy = remote(src, dst, other)
        copy.start()
        return copy

    half = steps // 2
    away = pl.multiple_of((1 - core) * half, 8)
    near = pl.multiple_of(core * half, 8)

    trans = trans_ref[...]
    trans_t = trans.T
    scaled_map = map_ref[...] * column(gain_ref[...], gain_ref.shape[1])
    keep = jnp.where(eye(width), 1.0, 0.0) - mm_first(scaled_map, map_ref[...])
    corr_t = mm(trans_t, keep)
    back_t = mm(trans, keep)
    ones = [trans_t, corr_t]
    both = jnp.concatenate(ones, 1)
    twos = mm(jnp.concatenate(ones, 0), both)
    pairs = [twos[a * width:(a + 1) * width, b * width:(b + 1) * width] for a in range(2) for b in range(2)]
    wide = jnp.concatenate(pairs, 1)
    for a in range(4):
        fours = mm(pairs[a], wide)
        for b in range(4):
            table[a * 4 + b] = fours[:, b * width:(b + 1) * width]

    pl.semaphore_wait(barrier, count - 1)
    obs_copy = send(obs_ref.at[0, pl.ds(away, half), :], got_obs, mate(1))
    flags[...] = jnp.broadcast_to(column(flag_ref[...].astype(F32), steps), flags.shape)
    obs_copy.wait_recv()
    own_push = mm_apply(obs_ref[0, pl.ds(near, half), :], scaled_map)
    got_push = mm_apply(got_obs[...], scaled_map)
    push[pl.ds(0, half, stride=2), :] = jnp.where(core == 0, own_push, got_push)
    push[pl.ds(1, half, stride=2), :] = jnp.where(core == 0, got_push, own_push)

    step_flags = [flags[pl.ds(j, chunks, stride=4), :] for j in range(4)]
    step_push = [push[pl.ds(j, chunks, stride=4), :] * step_flags[j] for j in range(4)]

    def advance(state, j, times=mm):
        moved = times(state, both)
        return jnp.where(step_flags[j] > 0, moved[:, width:], moved[:, :width]) + step_push[j]

    state = step_push[0]
    for j in range(1, 4):
        state = advance(state, j, mm_apply)

    def quad(q):
        f = [flag_smem[4 * q + j] for j in range(4)]
        return table[f[0] * 8 + f[1] * 4 + f[2] * 2 + f[3]]

    def spread(row):
        return jnp.broadcast_to(row, (8, width))

    def compose(early, late):
        moved = mm(jnp.concatenate(early, 0), late[0])
        return (moved[:width], moved[width:] + late[1])

    placed = [0]

    def keep_node(mat, vec):
        at = placed[0]
        placed[0] += 1
        held_tree[at, :width] = mat
        held_tree[at, width:] = vec
        return at

    def node(at):
        return (held_tree[at, :width], held_tree[at, width:])

    tree = [[keep_node(quad(q), spread(state[q:q + 1])) for q in range(chunks)]]
    while len(tree[-1]) > 1:
        ids = tree[-1]
        tree.append(
            [keep_node(*compose(node(ids[i]), node(ids[i + 1]))) for i in range(0, len(ids), 2)]
        )
    total = node(tree[-1][0])

    held_powers[0] = back_t
    powers = {1: 0}

    def power(n):
        if n not in powers:
            low = n // 2 if n & (n - 1) == 0 else n & -n
            value = mm(power(low), power(n - low))
            powers[n] = len(powers)
            held_powers[powers[n]] = value
        return held_powers[powers[n]]

    def read_map(ref):
        return (ref[:width], ref[width:])

    def pick(early, late, test):
        return tuple(jnp.where(test, a, b) for a, b in zip(early, late))

    def move(row, step_map):
        return mm(row, step_map[0]) + step_map[1]

    nothing = (jnp.where(eye(width), 1.0, 0.0), jnp.zeros((8, width), F32))
    own_map[:width] = total[0]
    own_map[width:] = total[1]
    copies = [send(own_map, core_map, mate(1))]
    mix_t = mm(trans_t, back_t)
    for n in (1, 2, 3, 4, 8):
        power(n)
    copies[-1].wait_recv()
    other_core = read_map(core_map)
    total = compose(pick(total, other_core, core == 0), pick(other_core, total, core == 0))
    chip = lax.rem(place // 2, 4)
    chip_maps[chip, :width] = total[0]
    chip_maps[chip, width:] = total[1]
    sent = [send(chip_maps.at[chip], chip_maps.at[chip], mate(mask)) for mask in (6, 2, 4)]
    copies += sent
    for n in (12, 16, 32, 48, 64, 128, 256, 512):
        power(n)
    for copy in sent:
        copy.wait_recv()
    maps = [read_map(chip_maps.at[i]) for i in range(4)]
    first_two = compose(maps[0], maps[1])
    all_four = compose(first_two, compose(maps[2], maps[3]))
    onward = remote(next_start, got_start, lax.rem(place + mates, count))

    @pl.when(line == 0)
    def _():
        start = spread(init_ref[...])
        got_start[...] = start
        next_start[...] = move(start, all_four)
        onward.start()

    before = pick(compose(first_two, maps[2]), first_two, chip == 3)
    before = pick(maps[0], before, chip == 1)
    before = pick(nothing, before, chip == 0)
    before = pick(compose(before, other_core), before, core == 1)
    tail_tiles = count // 8
    for n in list(range(1, 8)) + [8 * a for a in range(1, tail_tiles)]:
        power(n * steps)

    @pl.when(line > 0)
    def _():
        onward.wait_recv()

    @pl.when(jnp.logical_and(line > 0, line < lines - 1))
    def _():
        next_start[...] = move(got_start[...], all_four)
        onward.start()

    begin = move(got_start[...], before)

    heads = [begin]
    for ids in reversed(tree[:-1]):
        after = []
        for i, head in enumerate(heads):
            mat, vec = node(ids[2 * i])
            after.append(apply_row(head, mat) + vec)
        heads = [x for pair in zip(heads, after) for x in pair]
    lanes = lax.broadcasted_iota(jnp.int32, (8, width), 0)
    tiles = []
    for q in range(0, chunks, 8):
        tile = heads[q]
        for i in range(1, 8):
            tile = jnp.where(lanes == i, heads[q + i], tile)
        tiles.append(tile)
    state = jnp.concatenate(tiles, 0)
    for j in range(4):
        state = advance(state, j, mm_apply)
        push[pl.ds(j, chunks, stride=4), :] = state
    filtered = push[...]

    row_ids = lax.broadcasted_iota(jnp.int32, (steps, width), 0)
    final = jnp.logical_and(row_ids == steps - 1, place == last)
    blended = jnp.where(final, filtered, filtered - mm(filtered, mix_t))

    pad[steps:, :] = jnp.zeros((steps, width), F32)

    def suffixes(rows):
        stride = 1
        while stride < steps:
            pad[:steps, :] = rows
            moved = jnp.concatenate([pad[n * stride:n * stride + steps, :] for n in (1, 2, 3)], 1)
            rows = rows + mm_apply(moved, jnp.concatenate([power(n * stride) for n in (1, 2, 3)], 0))
            stride *= 4
        return rows

    partial = suffixes(blended)
    got_tails[last] = partial[:1]
    sent = [
        send(got_tails.at[last], got_tails.at[n], lax.rem(place + 2 * count - 1 - n, count))
        for n in range(last)
    ]
    copies += sent
    far = halves(jnp.concatenate([power(8 * a * steps) for a in range(1, tail_tiles)], 0))
    close = halves(jnp.concatenate([power(n * steps) for n in range(1, 8)], 0))
    for copy in sent:
        copy.wait_recv()
    order = lax.broadcasted_iota(jnp.int32, (count, width), 0)
    later = jnp.where(order < last - place, got_tails[:, 0, :], 0.0)
    folded = later[:8] + mm_halves(
        jnp.concatenate([later[8 * a:8 * a + 8] for a in range(1, tail_tiles)], 1), far
    )
    arriving = spread(folded[:1]) + mm_halves(
        jnp.concatenate([spread(folded[n:n + 1]) for n in range(1, 8)], 1), close
    )
    entry = jnp.where(row_ids == steps - 1, mm(arriving, back_t)[:1], 0.0)
    smoothed = partial + suffixes(entry)
    smooth_ref[...] = smoothed

    pad[:steps, :] = smoothed
    pad[steps:steps + 8, :] = arriving
    following = pad[1:steps + 1, :]
    counted = jnp.where(final, 0.0, smoothed)
    moments = mm_apply(counted.T, jnp.concatenate([smoothed, following], 1))
    owned = width // mates
    for n in range(mates):
        moment[n] = moments[n * owned:(n + 1) * owned]
    sent = [
        send(moment.at[lax.rem(mate(mask), mates)], got_moment.at[mask], mate(mask))
        for mask in (6, 7, 2, 3, 4, 5, 1)
    ]
    copies += sent
    pair_count = F32(steps * (last + 1) - 1)
    lag_t = pair_count * lax.dot_general(
        back_t, cov_ref[...], (((0,), (1,)), ((), ())),
        precision=lax.Precision.HIGHEST, preferred_element_type=F32,
    )
    for copy in sent:
        copy.wait_recv()
    held = moment[mine]
    for n in range(1, mates):
        held = held + got_moment[n]
    line_moment[line] = held
    sent = [
        send(line_moment.at[line], line_moment.at[line], lax.rem(place + mates * n, count))
        for n in range(1, lines)
    ]
    copies += sent
    for copy in sent:
        copy.wait_recv()
    held = line_moment[0]
    for n in range(1, lines):
        held = held + line_moment[n]
    full_moment[mine] = held
    sent = [
        send(full_moment.at[mine], full_moment.at[mine], mate(mask)) for mask in (6, 7, 2, 3, 4, 5, 1)
    ]
    copies += sent
    for copy in sent:
        copy.wait_recv()
    extra = jnp.concatenate([pair_count * cov_ref[...], lag_t], 1)
    for n in range(mates):
        rows = slice(n * owned, (n + 1) * owned)
        sums_ref[rows, :] = full_moment[n] + extra[rows]

    @pl.when(line < lines - 1)
    def _():
        onward.wait_send()

    obs_copy.wait_send()
    for copy in copies:
        copy.wait_send()


def product(x, y):
    return [
        [sum((x[i][k] * y[k][j] for k in range(1, len(y))), x[i][0] * y[0][j]) for j in range(len(y[0]))]
        for i in range(len(x))
    ]


def small_inverse(d):
    n = len(d)
    if n == 1:
        return [[1.0 / d[0][0]]]
    if n == 2:
        det = 1.0 / (d[0][0] * d[1][1] - d[0][1] * d[0][1])
        off = -d[0][1] * det
        return [[d[1][1] * det, off], [off, d[0][0] * det]]
    h = n // 2
    head = small_inverse([r[:h] for r in d[:h]])
    side = [r[h:] for r in d[:h]]
    spread = product(head, side)
    fill = product([list(x) for x in zip(*side)], spread)
    rest = small_inverse([[d[h + i][h + j] - fill[i][j] for j in range(h)] for i in range(h)])
    back = product(spread, rest)
    fill = product(back, [list(x) for x in zip(*spread)])
    top = [[head[i][j] + fill[i][j] for j in range(h)] + [-x for x in back[i]] for i in range(h)]
    return top + [[-back[j][i] for j in range(h)] + rest[i] for i in range(h)]


def combine(rows, weights):
    total = rows[0] * weights[0]
    for row, weight in zip(rows[1:], weights[1:]):
        total = total + row * weight
    return total


def solve_kernel(sums_ref, smooth_ref, out_ref, smooth_out_ref):
    smooth_out_ref[...] = smooth_ref[...]
    width = out_ref.shape[0]
    groups = width // 8
    per = 4
    full = (8, width)
    left = [sums_ref[8 * g:8 * g + 8, :width] for g in range(groups)]
    right = [sums_ref[8 * g:8 * g + 8, width:] for g in range(groups)]
    lane = lax.broadcasted_iota(jnp.int32, (1, width), 1)
    sub = lax.broadcasted_iota(jnp.int32, full, 0)

    def spread_row(tile, i):
        return jnp.broadcast_to(tile[i:i + 1, :], full)

    for at in range(0, groups, per):
        panel = range(at, at + per)
        for pivot in panel:
            cols = {
                g: [jnp.broadcast_to(left[g][:, k:k + 1], full) for k in range(8 * pivot, 8 * pivot + 8)]
                for g in panel
            }
            inverse = small_inverse(
                [[spread_row(cols[pivot][max(i, j)], min(i, j)) for j in range(8)] for i in range(8)]
            )
            for side in (left, right):
                rows = [spread_row(side[pivot], j) for j in range(8)]
                solved = [combine(rows, inverse[i]) for i in range(8)]
                for g in panel:
                    if g == pivot:
                        tile = solved[0]
                        for j in range(1, 8):
                            tile = jnp.where(sub == j, solved[j], tile)
                        side[g] = tile
                    else:
                        side[g] = side[g] - combine(cols[g], solved)
        mask = jnp.logical_and(lane >= 8 * at, lane < 8 * (at + per))
        order = [g % groups for g in range(at + per, at + groups)]
        rows = [jnp.concatenate([left[g], right[g]], 1) for g in panel]
        before, after = 8 * at, 8 * (groups - at - per)
        if before:
            rows = [jnp.zeros((before, 2 * width), F32)] + rows
        if after:
            rows = rows + [jnp.zeros((after, 2 * width), F32)]
        change = mm(
            jnp.concatenate([jnp.where(mask, left[g], 0.0) for g in order], 0), jnp.concatenate(rows, 0)
        )
        for i, g in enumerate(order):
            left[g] = left[g] - change[8 * i:8 * i + 8, :width]
            right[g] = right[g] - change[8 * i:8 * i + 8, width:]
    out_ref[...] = jnp.concatenate(right, 0).T


def local(levels, obs_store, observed, transition, obs_map, gain_weights, init_mean, smoothed_cov):
    steps = observed.shape[0]
    width = transition.shape[0]
    vmem = pl.BlockSpec(memory_space=pltpu.VMEM)
    smem = pl.BlockSpec(memory_space=pltpu.SMEM)
    count = 2**levels
    mates = 8
    copies = 1 + 1 + 3 + 1 + (count - 1) + 2 * (mates - 1) + (count // mates - 1)
    chip_map = (width + 8, width)
    owned = (width // mates, 2 * width)
    smoothed, sums = pl.pallas_call(
        functools.partial(em_kernel, levels),
        out_shape=(
            jax.ShapeDtypeStruct((steps, width), F32),
            jax.ShapeDtypeStruct((width, 2 * width), F32),
        ),
        in_specs=[vmem, smem, vmem, vmem, vmem, vmem, vmem, vmem],
        out_specs=(vmem, vmem),
        scratch_shapes=[
            pltpu.VMEM((steps // 2, obs_map.shape[0]), F32),
            pltpu.VMEM((16, width, width), F32),
            pltpu.VMEM((steps, width), F32),
            pltpu.VMEM((steps, width), F32),
            pltpu.VMEM((2 * steps, width), F32),
            pltpu.VMEM(chip_map, F32),
            pltpu.VMEM(chip_map, F32),
            pltpu.VMEM((4, *chip_map), F32),
            pltpu.VMEM((8, width), F32),
            pltpu.VMEM((8, width), F32),
            pltpu.VMEM((count, 1, width), F32),
            pltpu.VMEM((mates, *owned), F32),
            pltpu.VMEM((mates, *owned), F32),
            pltpu.VMEM((count // mates, *owned), F32),
            pltpu.VMEM((mates, *owned), F32),
            pltpu.VMEM((steps // 2 - 1, width + 8, width), F32),
            pltpu.VMEM((24 + count // 8, width, width), F32),
            pltpu.SemaphoreType.DMA((copies,)),
            pltpu.SemaphoreType.DMA((copies,)),
        ],
        compiler_params=pltpu.CompilerParams(collective_id=0, has_side_effects=True),
    )(
        obs_store, observed, observed.reshape(1, -1), transition, obs_map,
        gain_weights.reshape(1, -1), init_mean.reshape(1, -1), smoothed_cov,
    )
    new_transition, smoothed = pl.pallas_call(
        solve_kernel,
        out_shape=(
            jax.ShapeDtypeStruct((width, width), F32),
            jax.ShapeDtypeStruct((steps, width), F32),
        ),
        in_specs=[vmem, vmem],
        out_specs=(vmem, vmem),
    )(sums, smoothed)
    return (smoothed, new_transition)


def solution(mesh):
    levels = (mesh.shape["tm"] * mesh.shape["replay"]).bit_length() - 1
    return jax.shard_map(
        functools.partial(local, levels),
        mesh=mesh,
        in_specs=(P("replay", "tm", None), P(("tm", "replay")), P(), P(), P(), P(), P()),
        out_specs=(P(("tm", "replay"), None), P()),
        check_vma=False,
    )
```

```python
import functools

import jax
import jax.numpy as jnp
from jax import lax
from jax.experimental import pallas as pl
from jax.experimental.pallas import tpu as pltpu
from jax.sharding import PartitionSpec as P

MESH = pl.DeviceIdType.MESH
F32 = jnp.float32


def halves(a):
    high = a.astype(jnp.bfloat16)
    return high, (a - high.astype(F32)).astype(jnp.bfloat16)


def thirds(a):
    high = a.astype(jnp.bfloat16)
    rest = a - high.astype(F32)
    mid = rest.astype(jnp.bfloat16)
    return high, mid, (rest - mid.astype(F32)).astype(jnp.bfloat16)


def mm(a, b):
    width = b.shape[1]
    a_high, a_mid, a_low = thirds(a)
    b_high, b_mid, b_low = thirds(b)
    row = jnp.concatenate([b_high, b_mid], 1)
    large = jnp.dot(
        jnp.concatenate([a_high, a_mid], 1), jnp.concatenate([row, row], 0), preferred_element_type=F32
    )
    small = jnp.dot(
        jnp.concatenate([a_low, a_high], 1), jnp.concatenate([b_high, b_low], 0),
        preferred_element_type=F32,
    )
    return large[:, :width] + (large[:, width:] + small)


def mm_apply(a, b):
    if a.shape[1] == 128:
        return mm_packed(a, b)
    rows = a.shape[0]
    a_high, a_low = halves(a)
    b_high, b_low = halves(b)
    both = jnp.dot(jnp.concatenate([a_high, a_low], 0), b_high, preferred_element_type=F32)
    return both[:rows] + both[rows:] + jnp.dot(a_high, b_low, preferred_element_type=F32)


def mm_packed(a, b):
    width = b.shape[1]
    b_high, b_low = halves(b)
    lower = jnp.concatenate([b_high, jnp.zeros_like(b_low)], 1)
    weights = jnp.concatenate([jnp.concatenate([b_high, b_low], 1), lower], 0)
    out = jnp.dot(jnp.concatenate(halves(a), 1), weights, preferred_element_type=F32)
    return out[:, :width] + out[:, width:]


def mm_halves(a, b_halves):
    rows = a.shape[0]
    a_high, a_low = halves(a)
    both = jnp.dot(jnp.concatenate([a_high, a_low], 0), b_halves[0], preferred_element_type=F32)
    return both[:rows] + both[rows:] + jnp.dot(a_high, b_halves[1], preferred_element_type=F32)


def apply_row(row, mat):
    return mm_apply(jnp.concatenate([row, row], 0), mat)[:8]


def mm_first(a, b):
    return lax.dot_general(
        a, b, (((0,), (0,)), ((), ())), precision=lax.Precision.HIGHEST, preferred_element_type=F32
    )


def eye(n):
    rows = lax.broadcasted_iota(jnp.int32, (n, n), 0)
    return rows == lax.broadcasted_iota(jnp.int32, (n, n), 1)


def column(row, n):
    return jnp.sum(jnp.where(eye(n), jnp.broadcast_to(row, (n, n)), 0.0), axis=1, keepdims=True)


def flip(place, bit):
    return place + bit * (1 - 2 * lax.rem(place // bit, 2))


def em_kernel(
    levels, obs_ref, flag_smem, flag_ref, trans_ref, map_ref, gain_ref, init_ref, cov_ref,
    smooth_ref, sums_ref,
    got_obs, table, push, flags, pad, own_map, core_map, chip_maps, got_start, next_start, got_near,
    got_far, held_steps, held_jumps,
    moment, got_moment, line_moment, full_moment, held_tree, held_powers, send_sem, recv_sem,
):
    steps = push.shape[0]
    width = trans_ref.shape[0]
    chunks = steps // 4
    tm = lax.axis_index("tm")
    core = lax.axis_index("replay")
    place = tm * 2 + core
    count = 2**levels
    last = count - 1
    near_bits = 3
    mates = 2**near_bits
    lines = count // mates
    mine = lax.rem(place, mates)
    line = place // mates

    def at_place(other):
        return (other // 2, lax.rem(other, 2))

    def mate(mask):
        other = place
        for k in range(near_bits):
            if mask >> k & 1:
                other = flip(other, 2**k)
        return other

    others = [mate(mask) for mask in range(1, mates)]
    others += [lax.rem(place + mates * n, count) for n in range(1, lines)]
    barrier = pltpu.get_barrier_semaphore()
    for other in others:
        pl.semaphore_signal(barrier, inc=1, device_id=at_place(other), device_id_type=MESH)

    used = [0]

    def remote(src, dst, other):
        slot = used[0]
        used[0] += 1
        return pltpu.make_async_remote_copy(
            src_ref=src, dst_ref=dst, send_sem=send_sem.at[slot], recv_sem=recv_sem.at[slot],
            device_id=at_place(other), device_id_type=MESH,
        )

    def send(src, dst, other):
        copy = remote(src, dst, other)
        copy.start()
        return copy

    half = steps // 2
    away = pl.multiple_of((1 - core) * half, 8)
    near = pl.multiple_of(core * half, 8)

    trans = trans_ref[...]
    trans_t = trans.T
    scaled_map = map_ref[...] * column(gain_ref[...], gain_ref.shape[1])
    keep = jnp.where(eye(width), 1.0, 0.0) - mm_first(scaled_map, map_ref[...])
    corr_t = mm(trans_t, keep)
    back_t = mm(trans, keep)
    ones = [trans_t, corr_t]
    both = jnp.concatenate(ones, 1)
    twos = mm(jnp.concatenate(ones, 0), both)
    pairs = [twos[a * width:(a + 1) * width, b * width:(b + 1) * width] for a in range(2) for b in range(2)]
    wide = jnp.concatenate(pairs, 1)
    for a in range(4):
        fours = mm(pairs[a], wide)
        for b in range(4):
            table[a * 4 + b] = fours[:, b * width:(b + 1) * width]

    pl.semaphore_wait(barrier, len(others))
    obs_copy = send(obs_ref.at[0, pl.ds(away, half), :], got_obs, mate(1))
    flags[...] = jnp.broadcast_to(column(flag_ref[...].astype(F32), steps), flags.shape)
    obs_copy.wait_recv()
    own_push = mm_apply(obs_ref[0, pl.ds(near, half), :], scaled_map)
    got_push = mm_apply(got_obs[...], scaled_map)
    push[pl.ds(0, half, stride=2), :] = jnp.where(core == 0, own_push, got_push)
    push[pl.ds(1, half, stride=2), :] = jnp.where(core == 0, got_push, own_push)

    step_flags = [flags[pl.ds(j, chunks, stride=4), :] for j in range(4)]
    step_push = [push[pl.ds(j, chunks, stride=4), :] * step_flags[j] for j in range(4)]

    def advance(state, j, times=mm):
        moved = times(state, both)
        return jnp.where(step_flags[j] > 0, moved[:, width:], moved[:, :width]) + step_push[j]

    state = step_push[0]
    for j in range(1, 4):
        state = advance(state, j, mm_apply)

    def quad(q):
        f = [flag_smem[4 * q + j] for j in range(4)]
        return table[f[0] * 8 + f[1] * 4 + f[2] * 2 + f[3]]

    def spread(row):
        return jnp.broadcast_to(row, (8, width))

    def compose(early, late):
        moved = mm_packed(jnp.concatenate(early, 0), late[0])
        return (moved[:width], moved[width:] + late[1])

    placed = [0]

    def keep_node(mat, vec):
        at = placed[0]
        placed[0] += 1
        held_tree[at, :width] = mat
        held_tree[at, width:] = vec
        return at

    def node(at):
        return (held_tree[at, :width], held_tree[at, width:])

    tree = [[keep_node(quad(q), spread(state[q:q + 1])) for q in range(chunks)]]
    while len(tree[-1]) > 1:
        ids = tree[-1]
        tree.append(
            [keep_node(*compose(node(ids[i]), node(ids[i + 1]))) for i in range(0, len(ids), 2)]
        )
    total = node(tree[-1][0])

    held_powers[0] = back_t
    powers = {1: 0}

    def power(n):
        if n not in powers:
            low = n // 2 if n & (n - 1) == 0 else n & -n
            value = mm(power(low), power(n - low))
            powers[n] = len(powers)
            held_powers[powers[n]] = value
        return held_powers[powers[n]]

    def read_map(ref):
        return (ref[:width], ref[width:])

    def pick(early, late, test):
        return tuple(jnp.where(test, a, b) for a, b in zip(early, late))

    def move(row, step_map):
        return mm(row, step_map[0]) + step_map[1]

    nothing = (jnp.where(eye(width), 1.0, 0.0), jnp.zeros((8, width), F32))
    own_map[:width] = total[0]
    own_map[width:] = total[1]
    copies = [send(own_map, core_map, mate(1))]
    mix_t = mm(trans_t, back_t)
    for n in (1, 2, 3, 4, 8):
        power(n)
    copies[-1].wait_recv()
    other_core = read_map(core_map)
    total = compose(pick(total, other_core, core == 0), pick(other_core, total, core == 0))
    chip = lax.rem(place // 2, 4)
    chip_maps[chip, :width] = total[0]
    chip_maps[chip, width:] = total[1]
    sent = [send(chip_maps.at[chip], chip_maps.at[chip], mate(mask)) for mask in (6, 2, 4)]
    copies += sent
    for n in (12, 16, 32, 48, 64, 128, 256, 512):
        power(n)
    for copy in sent:
        copy.wait_recv()
    maps = [read_map(chip_maps.at[i]) for i in range(4)]
    first_two = compose(maps[0], maps[1])
    all_four = compose(first_two, compose(maps[2], maps[3]))
    onward = remote(next_start, got_start, lax.rem(place + mates, count))

    @pl.when(line == 0)
    def _():
        start = spread(init_ref[...])
        got_start[...] = start
        next_start[...] = move(start, all_four)
        onward.start()

    before = pick(compose(first_two, maps[2]), first_two, chip == 3)
    before = pick(maps[0], before, chip == 1)
    before = pick(nothing, before, chip == 0)
    before = pick(compose(before, other_core), before, core == 1)
    for n in list(range(1, mates)) + [mates * n for n in range(1, lines - 1)]:
        power(n * steps)
    across = nothing[0]
    for n in range(1, mates):
        across = jnp.where(mine == mates - 1 - n, power(n * steps), across)
    jumps = [across] + [mm(power(mates * n * steps), across) for n in range(1, lines - 1)]
    for n, jump in enumerate(jumps):
        held_jumps[n * width:(n + 1) * width] = jump
    for n in range(1, mates):
        held_steps[(n - 1) * width:n * width] = power(n * steps)

    @pl.when(line > 0)
    def _():
        onward.wait_recv()

    @pl.when(jnp.logical_and(line > 0, line < lines - 1))
    def _():
        next_start[...] = move(got_start[...], all_four)
        onward.start()

    begin = move(got_start[...], before)

    heads = [begin]
    for ids in reversed(tree[:-1]):
        after = []
        for i, head in enumerate(heads):
            mat, vec = node(ids[2 * i])
            after.append(apply_row(head, mat) + vec)
        heads = [x for pair in zip(heads, after) for x in pair]
    lanes = lax.broadcasted_iota(jnp.int32, (8, width), 0)
    tiles = []
    for q in range(0, chunks, 8):
        tile = heads[q]
        for i in range(1, 8):
            tile = jnp.where(lanes == i, heads[q + i], tile)
        tiles.append(tile)
    state = jnp.concatenate(tiles, 0)
    for j in range(4):
        state = advance(state, j, mm_apply)
        push[pl.ds(j, chunks, stride=4), :] = state
    filtered = push[...]

    row_ids = lax.broadcasted_iota(jnp.int32, (steps, width), 0)
    final = jnp.logical_and(row_ids == steps - 1, place == last)
    blended = jnp.where(final, filtered, filtered - mm(filtered, mix_t))

    pad[steps:, :] = jnp.zeros((steps, width), F32)

    def suffixes(rows):
        stride = 1
        while stride < steps:
            pad[:steps, :] = rows
            moved = jnp.concatenate([pad[n * stride:n * stride + steps, :] for n in (1, 2, 3)], 1)
            rows = rows + mm_apply(moved, jnp.concatenate([power(n * stride) for n in (1, 2, 3)], 0))
            stride *= 4
        return rows

    partial = suffixes(blended)
    got_near[mates:] = jnp.zeros((mates, 1, width), F32)
    got_near[mine] = partial[:1]
    sent = [send(got_near.at[mine], got_near.at[mine], mate(mask)) for mask in (6, 7, 2, 3, 4, 5, 1)]
    copies += sent
    steps_halves = halves(held_steps[...])
    for copy in sent:
        copy.wait_recv()
    rows = [got_near[n] for n in range(mates)]
    after = [got_near[mine + 1 + n] for n in range(mates)]
    both_rows = jnp.concatenate(
        [jnp.concatenate([spread(a), spread(b)], 0) for a, b in zip(rows[1:], after[1:])], 1
    )
    folded = mm_halves(both_rows, steps_halves)
    got_far[lines - 1] = folded[:1] + rows[0]
    tail = folded[8:] + spread(after[0])
    sent = [
        send(got_far.at[lines - 1], got_far.at[n], lax.rem(place + mates * (2 * lines - 1 - n), count))
        for n in range(lines - 1)
    ]
    copies += sent
    jumps_halves = halves(held_jumps[...])
    for copy in sent:
        copy.wait_recv()
    later = [
        jnp.where(n < lines - 1 - line, spread(got_far[n]), 0.0) for n in range(lines - 1)
    ]
    arriving = tail + mm_halves(jnp.concatenate(later, 1), jumps_halves)
    entry = jnp.where(row_ids == steps - 1, mm(arriving, back_t)[:1], 0.0)
    smoothed = partial + suffixes(entry)
    smooth_ref[...] = smoothed

    pad[:steps, :] = smoothed
    pad[steps:steps + 8, :] = arriving
    following = pad[1:steps + 1, :]
    counted = jnp.where(final, 0.0, smoothed)
    moments = mm_apply(counted.T, jnp.concatenate([smoothed, following], 1))
    owned = width // mates
    for n in range(mates):
        moment[n] = moments[n * owned:(n + 1) * owned]
    sent = [
        send(moment.at[lax.rem(mate(mask), mates)], got_moment.at[mask], mate(mask))
        for mask in (6, 7, 2, 3, 4, 5, 1)
    ]
    copies += sent
    pair_count = F32(steps * (last + 1) - 1)
    lag_t = pair_count * lax.dot_general(
        back_t, cov_ref[...], (((0,), (1,)), ((), ())),
        precision=lax.Precision.HIGHEST, preferred_element_type=F32,
    )
    for copy in sent:
        copy.wait_recv()
    held = moment[mine]
    for n in range(1, mates):
        held = held + got_moment[n]
    line_moment[line] = held
    sent = [
        send(line_moment.at[line], line_moment.at[line], lax.rem(place + mates * n, count))
        for n in range(1, lines)
    ]
    copies += sent
    for copy in sent:
        copy.wait_recv()
    held = line_moment[0]
    for n in range(1, lines):
        held = held + line_moment[n]
    full_moment[mine] = held
    sent = [
        send(full_moment.at[mine], full_moment.at[mine], mate(mask)) for mask in (6, 7, 2, 3, 4, 5, 1)
    ]
    copies += sent
    for copy in sent:
        copy.wait_recv()
    extra = jnp.concatenate([pair_count * cov_ref[...], lag_t], 1)
    for n in range(mates):
        rows = slice(n * owned, (n + 1) * owned)
        sums_ref[rows, :] = full_moment[n] + extra[rows]

    @pl.when(line < lines - 1)
    def _():
        onward.wait_send()

    obs_copy.wait_send()
    for copy in copies:
        copy.wait_send()


def product(x, y):
    return [
        [sum((x[i][k] * y[k][j] for k in range(1, len(y))), x[i][0] * y[0][j]) for j in range(len(y[0]))]
        for i in range(len(x))
    ]


def small_inverse(d):
    n = len(d)
    if n == 1:
        return [[1.0 / d[0][0]]]
    if n == 2:
        det = 1.0 / (d[0][0] * d[1][1] - d[0][1] * d[0][1])
        off = -d[0][1] * det
        return [[d[1][1] * det, off], [off, d[0][0] * det]]
    h = n // 2
    head = small_inverse([r[:h] for r in d[:h]])
    side = [r[h:] for r in d[:h]]
    spread = product(head, side)
    fill = product([list(x) for x in zip(*side)], spread)
    rest = small_inverse([[d[h + i][h + j] - fill[i][j] for j in range(h)] for i in range(h)])
    back = product(spread, rest)
    fill = product(back, [list(x) for x in zip(*spread)])
    top = [[head[i][j] + fill[i][j] for j in range(h)] + [-x for x in back[i]] for i in range(h)]
    return top + [[-back[j][i] for j in range(h)] + rest[i] for i in range(h)]


def combine(rows, weights):
    total = rows[0] * weights[0]
    for row, weight in zip(rows[1:], weights[1:]):
        total = total + row * weight
    return total


def solve_kernel(sums_ref, smooth_ref, out_ref, smooth_out_ref):
    smooth_out_ref[...] = smooth_ref[...]
    width = out_ref.shape[0]
    groups = width // 8
    per = 4
    full = (8, width)
    left = [sums_ref[8 * g:8 * g + 8, :width] for g in range(groups)]
    right = [sums_ref[8 * g:8 * g + 8, width:] for g in range(groups)]
    lane = lax.broadcasted_iota(jnp.int32, (1, width), 1)
    sub = lax.broadcasted_iota(jnp.int32, full, 0)

    def spread_row(tile, i):
        return jnp.broadcast_to(tile[i:i + 1, :], full)

    for at in range(0, groups, per):
        panel = range(at, at + per)
        for pivot in panel:
            cols = {
                g: [jnp.broadcast_to(left[g][:, k:k + 1], full) for k in range(8 * pivot, 8 * pivot + 8)]
                for g in panel
            }
            inverse = small_inverse(
                [[spread_row(cols[pivot][max(i, j)], min(i, j)) for j in range(8)] for i in range(8)]
            )
            for side in (left, right):
                rows = [spread_row(side[pivot], j) for j in range(8)]
                solved = [combine(rows, inverse[i]) for i in range(8)]
                for g in panel:
                    if g == pivot:
                        tile = solved[0]
                        for j in range(1, 8):
                            tile = jnp.where(sub == j, solved[j], tile)
                        side[g] = tile
                    else:
                        side[g] = side[g] - combine(cols[g], solved)
        mask = jnp.logical_and(lane >= 8 * at, lane < 8 * (at + per))
        order = [g % groups for g in range(at + per, at + groups)]
        rows = [jnp.concatenate([left[g], right[g]], 1) for g in panel]
        before, after = 8 * at, 8 * (groups - at - per)
        if before:
            rows = [jnp.zeros((before, 2 * width), F32)] + rows
        if after:
            rows = rows + [jnp.zeros((after, 2 * width), F32)]
        change = mm(
            jnp.concatenate([jnp.where(mask, left[g], 0.0) for g in order], 0), jnp.concatenate(rows, 0)
        )
        for i, g in enumerate(order):
            left[g] = left[g] - change[8 * i:8 * i + 8, :width]
            right[g] = right[g] - change[8 * i:8 * i + 8, width:]
    out_ref[...] = jnp.concatenate(right, 0).T


def local(levels, obs_store, observed, transition, obs_map, gain_weights, init_mean, smoothed_cov):
    steps = observed.shape[0]
    width = transition.shape[0]
    vmem = pl.BlockSpec(memory_space=pltpu.VMEM)
    smem = pl.BlockSpec(memory_space=pltpu.SMEM)
    count = 2**levels
    mates = 8
    lines = count // mates
    copies = 6 + 3 * (mates - 1) + 2 * (lines - 1)
    chip_map = (width + 8, width)
    owned = (width // mates, 2 * width)
    smoothed, sums = pl.pallas_call(
        functools.partial(em_kernel, levels),
        out_shape=(
            jax.ShapeDtypeStruct((steps, width), F32),
            jax.ShapeDtypeStruct((width, 2 * width), F32),
        ),
        in_specs=[vmem, smem, vmem, vmem, vmem, vmem, vmem, vmem],
        out_specs=(vmem, vmem),
        scratch_shapes=[
            pltpu.VMEM((steps // 2, obs_map.shape[0]), F32),
            pltpu.VMEM((16, width, width), F32),
            pltpu.VMEM((steps, width), F32),
            pltpu.VMEM((steps, width), F32),
            pltpu.VMEM((2 * steps, width), F32),
            pltpu.VMEM(chip_map, F32),
            pltpu.VMEM(chip_map, F32),
            pltpu.VMEM((4, *chip_map), F32),
            pltpu.VMEM((8, width), F32),
            pltpu.VMEM((8, width), F32),
            pltpu.VMEM((2 * mates, 1, width), F32),
            pltpu.VMEM((lines, 1, width), F32),
            pltpu.VMEM(((mates - 1) * width, width), F32),
            pltpu.VMEM(((lines - 1) * width, width), F32),
            pltpu.VMEM((mates, *owned), F32),
            pltpu.VMEM((mates, *owned), F32),
            pltpu.VMEM((lines, *owned), F32),
            pltpu.VMEM((mates, *owned), F32),
            pltpu.VMEM((steps // 2 - 1, width + 8, width), F32),
            pltpu.VMEM((24 + lines, width, width), F32),
            pltpu.SemaphoreType.DMA((copies,)),
            pltpu.SemaphoreType.DMA((copies,)),
        ],
        compiler_params=pltpu.CompilerParams(collective_id=0, has_side_effects=True),
    )(
        obs_store, observed, observed.reshape(1, -1), transition, obs_map,
        gain_weights.reshape(1, -1), init_mean.reshape(1, -1), smoothed_cov,
    )
    new_transition, smoothed = pl.pallas_call(
        solve_kernel,
        out_shape=(
            jax.ShapeDtypeStruct((width, width), F32),
            jax.ShapeDtypeStruct((steps, width), F32),
        ),
        in_specs=[vmem, vmem],
        out_specs=(vmem, vmem),
    )(sums, smoothed)
    return (smoothed, new_transition)


def solution(mesh):
    levels = (mesh.shape["tm"] * mesh.shape["replay"]).bit_length() - 1
    return jax.shard_map(
        functools.partial(local, levels),
        mesh=mesh,
        in_specs=(P("replay", "tm", None), P(("tm", "replay")), P(), P(), P(), P(), P()),
        out_specs=(P(("tm", "replay"), None), P()),
        check_vma=False,
    )
```

```python
import functools

import jax
import jax.numpy as jnp
from jax import lax
from jax.experimental import pallas as pl
from jax.experimental.pallas import tpu as pltpu
from jax.sharding import PartitionSpec as P

MESH = pl.DeviceIdType.MESH
F32 = jnp.float32


def halves(a):
    high = a.astype(jnp.bfloat16)
    return high, (a - high.astype(F32)).astype(jnp.bfloat16)


def thirds(a):
    high = a.astype(jnp.bfloat16)
    rest = a - high.astype(F32)
    mid = rest.astype(jnp.bfloat16)
    return high, mid, (rest - mid.astype(F32)).astype(jnp.bfloat16)


def weights_of(b):
    high, mid, low = thirds(b)
    row = jnp.concatenate([high, mid], 1)
    return jnp.concatenate([row, row], 0), jnp.concatenate([high, low], 0)


def mm_weights(a, weights):
    width = weights[1].shape[1]
    high, mid, low = thirds(a)
    large = jnp.dot(jnp.concatenate([high, mid], 1), weights[0], preferred_element_type=F32)
    small = jnp.dot(jnp.concatenate([low, high], 1), weights[1], preferred_element_type=F32)
    return large[:, :width] + (large[:, width:] + small)


def mm(a, b):
    return mm_weights(a, weights_of(b))


def mm_apply(a, b):
    if a.shape[1] == 128:
        return mm_packed(a, b)
    rows = a.shape[0]
    a_high, a_low = halves(a)
    b_high, b_low = halves(b)
    both = jnp.dot(jnp.concatenate([a_high, a_low], 0), b_high, preferred_element_type=F32)
    return both[:rows] + both[rows:] + jnp.dot(a_high, b_low, preferred_element_type=F32)


def mm_packed(a, b):
    width = b.shape[1]
    b_high, b_low = halves(b)
    lower = jnp.concatenate([b_high, jnp.zeros_like(b_low)], 1)
    weights = jnp.concatenate([jnp.concatenate([b_high, b_low], 1), lower], 0)
    out = jnp.dot(jnp.concatenate(halves(a), 1), weights, preferred_element_type=F32)
    return out[:, :width] + out[:, width:]


def mm_halves(a, b_halves):
    rows = a.shape[0]
    a_high, a_low = halves(a)
    both = jnp.dot(jnp.concatenate([a_high, a_low], 0), b_halves[0], preferred_element_type=F32)
    return both[:rows] + both[rows:] + jnp.dot(a_high, b_halves[1], preferred_element_type=F32)


def apply_row(row, mat):
    return mm_apply(jnp.concatenate([row, row], 0), mat)[:8]


def mm_first(a, b):
    return lax.dot_general(
        a, b, (((0,), (0,)), ((), ())), precision=lax.Precision.HIGHEST, preferred_element_type=F32
    )


def eye(n):
    rows = lax.broadcasted_iota(jnp.int32, (n, n), 0)
    return rows == lax.broadcasted_iota(jnp.int32, (n, n), 1)


def column(row, n):
    return jnp.sum(jnp.where(eye(n), jnp.broadcast_to(row, (n, n)), 0.0), axis=1, keepdims=True)


def flip(place, bit):
    return place + bit * (1 - 2 * lax.rem(place // bit, 2))


def em_kernel(
    levels, obs_in, flag_in, flag_row_in, trans_in, map_in, gain_in, init_in, cov_in,
    smooth_ref, sums_ref,
    obs_ref, flag_smem, flag_ref, trans_ref, map_ref, gain_ref, init_ref, cov_ref, load_sem,
    got_obs, table, push, flags, pad, own_map, core_map, chip_maps, got_start, next_start, got_near,
    got_far, held_steps, held_jumps,
    moment, got_moment, line_moment, full_moment, held_tree, held_powers, send_sem, recv_sem,
):
    pairs_in = [
        (trans_in, trans_ref), (map_in, map_ref), (gain_in, gain_ref), (obs_in, obs_ref),
        (flag_row_in, flag_ref), (flag_in, flag_smem), (init_in, init_ref), (cov_in, cov_ref),
    ]
    loads = [
        pltpu.make_async_copy(source, place_ref, load_sem.at[i])
        for i, (source, place_ref) in enumerate(pairs_in)
    ]
    for load in loads:
        load.start()
    steps = push.shape[0]
    width = trans_ref.shape[0]
    chunks = steps // 4
    tm = lax.axis_index("tm")
    core = lax.axis_index("replay")
    place = tm * 2 + core
    count = 2**levels
    last = count - 1
    near_bits = 3
    mates = 2**near_bits
    lines = count // mates
    mine = lax.rem(place, mates)
    line = place // mates

    def at_place(other):
        return (other // 2, lax.rem(other, 2))

    def mate(mask):
        other = place
        for k in range(near_bits):
            if mask >> k & 1:
                other = flip(other, 2**k)
        return other

    others = [mate(mask) for mask in range(1, mates)]
    others += [lax.rem(place + mates * n, count) for n in range(1, lines)]
    barrier = pltpu.get_barrier_semaphore()
    for other in others:
        pl.semaphore_signal(barrier, inc=1, device_id=at_place(other), device_id_type=MESH)

    used = [0]

    def remote(src, dst, other):
        slot = used[0]
        used[0] += 1
        return pltpu.make_async_remote_copy(
            src_ref=src, dst_ref=dst, send_sem=send_sem.at[slot], recv_sem=recv_sem.at[slot],
            device_id=at_place(other), device_id_type=MESH,
        )

    def send(src, dst, other):
        copy = remote(src, dst, other)
        copy.start()
        return copy

    half = steps // 2
    away = pl.multiple_of((1 - core) * half, 8)
    near = pl.multiple_of(core * half, 8)

    for load in loads[:3]:
        load.wait()
    trans = trans_ref[...]
    trans_t = trans.T
    scaled_map = map_ref[...] * column(gain_ref[...], gain_ref.shape[1])
    keep = jnp.where(eye(width), 1.0, 0.0) - mm_first(scaled_map, map_ref[...])
    corr_t = mm(trans_t, keep)
    back_t = mm(trans, keep)
    ones = [trans_t, corr_t]
    both = jnp.concatenate(ones, 1)
    twos = mm(jnp.concatenate(ones, 0), both)
    pairs = [twos[a * width:(a + 1) * width, b * width:(b + 1) * width] for a in range(2) for b in range(2)]
    wide = jnp.concatenate(pairs, 1)
    for a in range(4):
        fours = mm(pairs[a], wide)
        for b in range(4):
            table[a * 4 + b] = fours[:, b * width:(b + 1) * width]

    for load in loads[3:]:
        load.wait()
    pl.semaphore_wait(barrier, len(others))
    obs_copy = send(obs_ref.at[0, pl.ds(away, half), :], got_obs, mate(1))
    flags[...] = jnp.broadcast_to(column(flag_ref[...].astype(F32), steps), flags.shape)
    obs_copy.wait_recv()
    own_push = mm_apply(obs_ref[0, pl.ds(near, half), :], scaled_map)
    got_push = mm_apply(got_obs[...], scaled_map)
    push[pl.ds(0, half, stride=2), :] = jnp.where(core == 0, own_push, got_push)
    push[pl.ds(1, half, stride=2), :] = jnp.where(core == 0, got_push, own_push)

    step_flags = [flags[pl.ds(j, chunks, stride=4), :] for j in range(4)]
    step_push = [push[pl.ds(j, chunks, stride=4), :] * step_flags[j] for j in range(4)]

    def advance(state, j, times=mm):
        moved = times(state, both)
        return jnp.where(step_flags[j] > 0, moved[:, width:], moved[:, :width]) + step_push[j]

    state = step_push[0]
    for j in range(1, 4):
        state = advance(state, j, mm_apply)

    def quad(q):
        f = [flag_smem[4 * q + j] for j in range(4)]
        return table[f[0] * 8 + f[1] * 4 + f[2] * 2 + f[3]]

    def spread(row):
        return jnp.broadcast_to(row, (8, width))

    def compose(early, late):
        moved = mm_packed(jnp.concatenate(early, 0), late[0])
        return (moved[:width], moved[width:] + late[1])

    placed = [0]

    def keep_node(mat, vec):
        at = placed[0]
        placed[0] += 1
        held_tree[at, :width] = mat
        held_tree[at, width:] = vec
        return at

    def node(at):
        return (held_tree[at, :width], held_tree[at, width:])

    tree = [[keep_node(quad(q), spread(state[q:q + 1])) for q in range(chunks)]]
    while len(tree[-1]) > 1:
        ids = tree[-1]
        tree.append(
            [keep_node(*compose(node(ids[i]), node(ids[i + 1]))) for i in range(0, len(ids), 2)]
        )
    total = node(tree[-1][0])

    held_powers[0] = back_t
    powers = {1: 0}

    def power(n):
        if n not in powers:
            low = n // 2 if n & (n - 1) == 0 else n & -n
            value = mm(power(low), power(n - low))
            powers[n] = len(powers)
            held_powers[powers[n]] = value
        return held_powers[powers[n]]

    def read_map(ref):
        return (ref[:width], ref[width:])

    def pick(early, late, test):
        return tuple(jnp.where(test, a, b) for a, b in zip(early, late))

    nothing = (jnp.where(eye(width), 1.0, 0.0), jnp.zeros((8, width), F32))
    own_map[:width] = total[0]
    own_map[width:] = total[1]
    copies = [send(own_map, core_map, mate(1))]
    mix_t = mm(trans_t, back_t)
    for n in (1, 2, 3, 4, 8):
        power(n)
    copies[-1].wait_recv()
    other_core = read_map(core_map)
    total = compose(pick(total, other_core, core == 0), pick(other_core, total, core == 0))
    chip = lax.rem(place // 2, 4)
    chip_maps[chip, :width] = total[0]
    chip_maps[chip, width:] = total[1]
    sent = [send(chip_maps.at[chip], chip_maps.at[chip], mate(mask)) for mask in (6, 2, 4)]
    copies += sent
    for n in (12, 16, 32, 48, 64, 128, 256, 512):
        power(n)
    for copy in sent:
        copy.wait_recv()
    maps = [read_map(chip_maps.at[i]) for i in range(4)]
    first_two = compose(maps[0], maps[1])
    all_four = compose(first_two, compose(maps[2], maps[3]))
    onward = remote(next_start, got_start, lax.rem(place + mates, count))

    plane_weights = weights_of(all_four[0])
    origin = spread(init_ref[...])
    beyond = mm_weights(origin, plane_weights) + all_four[1]

    @pl.when(line == 0)
    def _():
        got_start[...] = origin
        next_start[...] = beyond
        onward.start()

    before = pick(compose(first_two, maps[2]), first_two, chip == 3)
    before = pick(maps[0], before, chip == 1)
    before = pick(nothing, before, chip == 0)
    before = pick(compose(before, other_core), before, core == 1)
    for n in list(range(1, mates)) + [mates * n for n in range(1, lines - 1)]:
        power(n * steps)
    across = nothing[0]
    for n in range(1, mates):
        across = jnp.where(mine == mates - 1 - n, power(n * steps), across)
    jumps = [across] + [mm(power(mates * n * steps), across) for n in range(1, lines - 1)]
    for n, jump in enumerate(jumps):
        held_jumps[n * width:(n + 1) * width] = jump
    for n in range(1, mates):
        held_steps[(n - 1) * width:n * width] = power(n * steps)

    before_weights = weights_of(before[0])

    @pl.when(line > 0)
    def _():
        onward.wait_recv()

    start = got_start[...]
    beyond = mm_weights(start, plane_weights) + all_four[1]

    @pl.when(jnp.logical_and(line > 0, line < lines - 1))
    def _():
        next_start[...] = beyond
        onward.start()

    begin = mm_weights(start, before_weights) + before[1]

    heads = [begin]
    for ids in reversed(tree[:-1]):
        after = []
        for i, head in enumerate(heads):
            mat, vec = node(ids[2 * i])
            after.append(apply_row(head, mat) + vec)
        heads = [x for pair in zip(heads, after) for x in pair]
    lanes = lax.broadcasted_iota(jnp.int32, (8, width), 0)
    tiles = []
    for q in range(0, chunks, 8):
        tile = heads[q]
        for i in range(1, 8):
            tile = jnp.where(lanes == i, heads[q + i], tile)
        tiles.append(tile)
    state = jnp.concatenate(tiles, 0)
    for j in range(4):
        state = advance(state, j, mm_apply)
        push[pl.ds(j, chunks, stride=4), :] = state
    filtered = push[...]

    row_ids = lax.broadcasted_iota(jnp.int32, (steps, width), 0)
    final = jnp.logical_and(row_ids == steps - 1, place == last)
    blended = jnp.where(final, filtered, filtered - mm(filtered, mix_t))

    pad[steps:, :] = jnp.zeros((steps, width), F32)

    def suffixes(rows):
        stride = 1
        while stride < steps:
            pad[:steps, :] = rows
            moved = jnp.concatenate([pad[n * stride:n * stride + steps, :] for n in (1, 2, 3)], 1)
            rows = rows + mm_apply(moved, jnp.concatenate([power(n * stride) for n in (1, 2, 3)], 0))
            stride *= 4
        return rows

    partial = suffixes(blended)
    got_near[mates:] = jnp.zeros((mates, 1, width), F32)
    got_near[mine] = partial[:1]
    sent = [send(got_near.at[mine], got_near.at[mine], mate(mask)) for mask in (6, 7, 2, 3, 4, 5, 1)]
    copies += sent
    steps_halves = halves(held_steps[...])
    for copy in sent:
        copy.wait_recv()
    rows = [got_near[n] for n in range(mates)]
    after = [got_near[mine + 1 + n] for n in range(mates)]
    both_rows = jnp.concatenate(
        [jnp.concatenate([spread(a), spread(b)], 0) for a, b in zip(rows[1:], after[1:])], 1
    )
    folded = mm_halves(both_rows, steps_halves)
    got_far[lines - 1] = folded[:1] + rows[0]
    tail = folded[8:] + spread(after[0])
    sent = [
        send(got_far.at[lines - 1], got_far.at[n], lax.rem(place + mates * (2 * lines - 1 - n), count))
        for n in range(lines - 1)
    ]
    copies += sent
    jumps_halves = halves(held_jumps[...])
    for copy in sent:
        copy.wait_recv()
    later = [
        jnp.where(n < lines - 1 - line, spread(got_far[n]), 0.0) for n in range(lines - 1)
    ]
    arriving = tail + mm_halves(jnp.concatenate(later, 1), jumps_halves)
    entry = jnp.where(row_ids == steps - 1, mm(arriving, back_t)[:1], 0.0)
    smoothed = partial + suffixes(entry)
    smooth_ref[...] = smoothed

    pad[:steps, :] = smoothed
    pad[steps:steps + 8, :] = arriving
    following = pad[1:steps + 1, :]
    counted = jnp.where(final, 0.0, smoothed)
    moments = mm_apply(counted.T, jnp.concatenate([smoothed, following], 1))
    owned = width // mates
    for n in range(mates):
        moment[n] = moments[n * owned:(n + 1) * owned]
    sent = [
        send(moment.at[lax.rem(mate(mask), mates)], got_moment.at[mask], mate(mask))
        for mask in (6, 7, 2, 3, 4, 5, 1)
    ]
    copies += sent
    pair_count = F32(steps * (last + 1) - 1)
    lag_t = pair_count * lax.dot_general(
        back_t, cov_ref[...], (((0,), (1,)), ((), ())),
        precision=lax.Precision.HIGHEST, preferred_element_type=F32,
    )
    for copy in sent:
        copy.wait_recv()
    held = moment[mine]
    for n in range(1, mates):
        held = held + got_moment[n]
    line_moment[line] = held
    sent = [
        send(line_moment.at[line], line_moment.at[line], lax.rem(place + mates * n, count))
        for n in range(1, lines)
    ]
    copies += sent
    for copy in sent:
        copy.wait_recv()
    held = line_moment[0]
    for n in range(1, lines):
        held = held + line_moment[n]
    full_moment[mine] = held
    sent = [
        send(full_moment.at[mine], full_moment.at[mine], mate(mask)) for mask in (6, 7, 2, 3, 4, 5, 1)
    ]
    copies += sent
    for copy in sent:
        copy.wait_recv()
    extra = jnp.concatenate([pair_count * cov_ref[...], lag_t], 1)
    for n in range(mates):
        rows = slice(n * owned, (n + 1) * owned)
        sums_ref[rows, :] = full_moment[n] + extra[rows]

    @pl.when(line < lines - 1)
    def _():
        onward.wait_send()

    obs_copy.wait_send()
    for copy in copies:
        copy.wait_send()


def product(x, y):
    return [
        [sum((x[i][k] * y[k][j] for k in range(1, len(y))), x[i][0] * y[0][j]) for j in range(len(y[0]))]
        for i in range(len(x))
    ]


def small_inverse(d):
    n = len(d)
    if n == 1:
        return [[1.0 / d[0][0]]]
    if n == 2:
        det = 1.0 / (d[0][0] * d[1][1] - d[0][1] * d[0][1])
        off = -d[0][1] * det
        return [[d[1][1] * det, off], [off, d[0][0] * det]]
    h = n // 2
    head = small_inverse([r[:h] for r in d[:h]])
    side = [r[h:] for r in d[:h]]
    spread = product(head, side)
    fill = product([list(x) for x in zip(*side)], spread)
    rest = small_inverse([[d[h + i][h + j] - fill[i][j] for j in range(h)] for i in range(h)])
    back = product(spread, rest)
    fill = product(back, [list(x) for x in zip(*spread)])
    top = [[head[i][j] + fill[i][j] for j in range(h)] + [-x for x in back[i]] for i in range(h)]
    return top + [[-back[j][i] for j in range(h)] + rest[i] for i in range(h)]


def combine(rows, weights):
    total = rows[0] * weights[0]
    for row, weight in zip(rows[1:], weights[1:]):
        total = total + row * weight
    return total


def solve_kernel(sums_ref, smooth_ref, out_ref, smooth_out_ref):
    smooth_out_ref[...] = smooth_ref[...]
    width = out_ref.shape[0]
    groups = width // 8
    per = 4
    full = (8, width)
    left = [sums_ref[8 * g:8 * g + 8, :width] for g in range(groups)]
    right = [sums_ref[8 * g:8 * g + 8, width:] for g in range(groups)]
    lane = lax.broadcasted_iota(jnp.int32, (1, width), 1)
    sub = lax.broadcasted_iota(jnp.int32, full, 0)

    def spread_row(tile, i):
        return jnp.broadcast_to(tile[i:i + 1, :], full)

    for at in range(0, groups, per):
        panel = range(at, at + per)
        for pivot in panel:
            cols = {
                g: [jnp.broadcast_to(left[g][:, k:k + 1], full) for k in range(8 * pivot, 8 * pivot + 8)]
                for g in panel
            }
            inverse = small_inverse(
                [[spread_row(cols[pivot][max(i, j)], min(i, j)) for j in range(8)] for i in range(8)]
            )
            for side in (left, right):
                rows = [spread_row(side[pivot], j) for j in range(8)]
                solved = [combine(rows, inverse[i]) for i in range(8)]
                for g in panel:
                    if g == pivot:
                        tile = solved[0]
                        for j in range(1, 8):
                            tile = jnp.where(sub == j, solved[j], tile)
                        side[g] = tile
                    else:
                        side[g] = side[g] - combine(cols[g], solved)
        mask = jnp.logical_and(lane >= 8 * at, lane < 8 * (at + per))
        order = [g % groups for g in range(at + per, at + groups)]
        rows = [jnp.concatenate([left[g], right[g]], 1) for g in panel]
        before, after = 8 * at, 8 * (groups - at - per)
        if before:
            rows = [jnp.zeros((before, 2 * width), F32)] + rows
        if after:
            rows = rows + [jnp.zeros((after, 2 * width), F32)]
        change = mm(
            jnp.concatenate([jnp.where(mask, left[g], 0.0) for g in order], 0), jnp.concatenate(rows, 0)
        )
        for i, g in enumerate(order):
            left[g] = left[g] - change[8 * i:8 * i + 8, :width]
            right[g] = right[g] - change[8 * i:8 * i + 8, width:]
    out_ref[...] = jnp.concatenate(right, 0).T


def local(levels, obs_store, observed, transition, obs_map, gain_weights, init_mean, smoothed_cov):
    steps = observed.shape[0]
    width = transition.shape[0]
    vmem = pl.BlockSpec(memory_space=pltpu.VMEM)
    count = 2**levels
    mates = 8
    lines = count // mates
    copies = 6 + 3 * (mates - 1) + 2 * (lines - 1)
    chip_map = (width + 8, width)
    owned = (width // mates, 2 * width)
    smoothed, sums = pl.pallas_call(
        functools.partial(em_kernel, levels),
        out_shape=(
            jax.ShapeDtypeStruct((steps, width), F32),
            jax.ShapeDtypeStruct((width, 2 * width), F32),
        ),
        in_specs=[pl.BlockSpec(memory_space=pltpu.HBM)] * 8,
        out_specs=(vmem, vmem),
        scratch_shapes=[
            pltpu.VMEM(obs_store.shape, F32),
            pltpu.SMEM((steps,), jnp.int32),
            pltpu.VMEM((1, steps), jnp.int32),
            pltpu.VMEM((width, width), F32),
            pltpu.VMEM(obs_map.shape, F32),
            pltpu.VMEM((1, obs_map.shape[0]), F32),
            pltpu.VMEM((1, width), F32),
            pltpu.VMEM((width, width), F32),
            pltpu.SemaphoreType.DMA((8,)),
            pltpu.VMEM((steps // 2, obs_map.shape[0]), F32),
            pltpu.VMEM((16, width, width), F32),
            pltpu.VMEM((steps, width), F32),
            pltpu.VMEM((steps, width), F32),
            pltpu.VMEM((2 * steps, width), F32),
            pltpu.VMEM(chip_map, F32),
            pltpu.VMEM(chip_map, F32),
            pltpu.VMEM((4, *chip_map), F32),
            pltpu.VMEM((8, width), F32),
            pltpu.VMEM((8, width), F32),
            pltpu.VMEM((2 * mates, 1, width), F32),
            pltpu.VMEM((lines, 1, width), F32),
            pltpu.VMEM(((mates - 1) * width, width), F32),
            pltpu.VMEM(((lines - 1) * width, width), F32),
            pltpu.VMEM((mates, *owned), F32),
            pltpu.VMEM((mates, *owned), F32),
            pltpu.VMEM((lines, *owned), F32),
            pltpu.VMEM((mates, *owned), F32),
            pltpu.VMEM((steps // 2 - 1, width + 8, width), F32),
            pltpu.VMEM((24 + lines, width, width), F32),
            pltpu.SemaphoreType.DMA((copies,)),
            pltpu.SemaphoreType.DMA((copies,)),
        ],
        compiler_params=pltpu.CompilerParams(
            collective_id=0, has_side_effects=True, vmem_limit_bytes=24 * 2**20
        ),
    )(*[
        pltpu.with_memory_space_constraint(x, pltpu.HBM)
        for x in (
            obs_store, observed, observed.reshape(1, -1), transition, obs_map,
            gain_weights.reshape(1, -1), init_mean.reshape(1, -1), smoothed_cov,
        )
    ])
    new_transition, smoothed = pl.pallas_call(
        solve_kernel,
        out_shape=(
            jax.ShapeDtypeStruct((width, width), F32),
            jax.ShapeDtypeStruct((steps, width), F32),
        ),
        in_specs=[vmem, vmem],
        out_specs=(vmem, vmem),
        compiler_params=pltpu.CompilerParams(vmem_limit_bytes=24 * 2**20),
    )(sums, smoothed)
    return (smoothed, new_transition)


def solution(mesh):
    levels = (mesh.shape["tm"] * mesh.shape["replay"]).bit_length() - 1
    return jax.shard_map(
        functools.partial(local, levels),
        mesh=mesh,
        in_specs=(P("replay", "tm", None), P(("tm", "replay")), P(), P(), P(), P(), P()),
        out_specs=(P(("tm", "replay"), None), P()),
        check_vma=False,
    )
```

```python
import functools

import jax
import jax.numpy as jnp
from jax import lax
from jax.experimental import pallas as pl
from jax.experimental.pallas import tpu as pltpu
from jax.sharding import PartitionSpec as P

MESH = pl.DeviceIdType.MESH
F32 = jnp.float32


def halves(a):
    high = a.astype(jnp.bfloat16)
    return high, (a - high.astype(F32)).astype(jnp.bfloat16)


def thirds(a):
    high = a.astype(jnp.bfloat16)
    rest = a - high.astype(F32)
    mid = rest.astype(jnp.bfloat16)
    return high, mid, (rest - mid.astype(F32)).astype(jnp.bfloat16)


def weights_of(b):
    high, mid, low = thirds(b)
    row = jnp.concatenate([high, mid], 1)
    return jnp.concatenate([row, row], 0), jnp.concatenate([high, low], 0)


def mm_weights(a, weights):
    width = weights[1].shape[1]
    high, mid, low = thirds(a)
    large = jnp.dot(jnp.concatenate([high, mid], 1), weights[0], preferred_element_type=F32)
    small = jnp.dot(jnp.concatenate([low, high], 1), weights[1], preferred_element_type=F32)
    return large[:, :width] + (large[:, width:] + small)


def mm(a, b):
    return mm_weights(a, weights_of(b))


def mm_apply(a, b):
    if a.shape[1] == 128:
        return mm_packed(a, b)
    rows = a.shape[0]
    a_high, a_low = halves(a)
    b_high, b_low = halves(b)
    both = jnp.dot(jnp.concatenate([a_high, a_low], 0), b_high, preferred_element_type=F32)
    return both[:rows] + both[rows:] + jnp.dot(a_high, b_low, preferred_element_type=F32)


def mm_packed(a, b):
    width = b.shape[1]
    b_high, b_low = halves(b)
    lower = jnp.concatenate([b_high, jnp.zeros_like(b_low)], 1)
    weights = jnp.concatenate([jnp.concatenate([b_high, b_low], 1), lower], 0)
    out = jnp.dot(jnp.concatenate(halves(a), 1), weights, preferred_element_type=F32)
    return out[:, :width] + out[:, width:]


def mm_halves(a, b_halves):
    rows = a.shape[0]
    a_high, a_low = halves(a)
    both = jnp.dot(jnp.concatenate([a_high, a_low], 0), b_halves[0], preferred_element_type=F32)
    return both[:rows] + both[rows:] + jnp.dot(a_high, b_halves[1], preferred_element_type=F32)


def apply_row(row, mat):
    return mm_apply(jnp.concatenate([row, row], 0), mat)[:8]


def mm_first(a, b):
    return lax.dot_general(
        a, b, (((0,), (0,)), ((), ())), precision=lax.Precision.HIGHEST, preferred_element_type=F32
    )


def eye(n):
    rows = lax.broadcasted_iota(jnp.int32, (n, n), 0)
    return rows == lax.broadcasted_iota(jnp.int32, (n, n), 1)


def column(row, n):
    return jnp.sum(jnp.where(eye(n), jnp.broadcast_to(row, (n, n)), 0.0), axis=1, keepdims=True)


def flip(place, bit):
    return place + bit * (1 - 2 * lax.rem(place // bit, 2))


def em_kernel(
    levels, obs_in, flag_in, flag_row_in, trans_in, map_in, gain_in, init_in, cov_in,
    smooth_ref, sums_ref,
    obs_ref, flag_smem, flag_ref, trans_ref, map_ref, gain_ref, init_ref, cov_ref, load_sem,
    got_obs, table, push, flags, pad, own_map, core_map, chip_maps, got_start, next_start, got_leap, own_plane,
    got_plane, got_near,
    got_far, held_steps, held_jumps,
    moment, got_moment, line_moment, full_moment, held_tree, held_powers, send_sem, recv_sem,
):
    pairs_in = [
        (trans_in, trans_ref), (map_in, map_ref), (gain_in, gain_ref), (obs_in, obs_ref),
        (flag_row_in, flag_ref), (flag_in, flag_smem), (init_in, init_ref), (cov_in, cov_ref),
    ]
    loads = [
        pltpu.make_async_copy(source, place_ref, load_sem.at[i])
        for i, (source, place_ref) in enumerate(pairs_in)
    ]
    for load in loads:
        load.start()
    steps = push.shape[0]
    width = trans_ref.shape[0]
    chunks = steps // 4
    tm = lax.axis_index("tm")
    core = lax.axis_index("replay")
    place = tm * 2 + core
    count = 2**levels
    last = count - 1
    near_bits = 3
    mates = 2**near_bits
    lines = count // mates
    mine = lax.rem(place, mates)
    line = place // mates

    def at_place(other):
        return (other // 2, lax.rem(other, 2))

    def mate(mask):
        other = place
        for k in range(near_bits):
            if mask >> k & 1:
                other = flip(other, 2**k)
        return other

    others = [mate(mask) for mask in range(1, mates)]
    others += [lax.rem(place + mates * n, count) for n in range(1, lines)]
    barrier = pltpu.get_barrier_semaphore()
    for other in others:
        pl.semaphore_signal(barrier, inc=1, device_id=at_place(other), device_id_type=MESH)

    used = [0]

    def remote(src, dst, other):
        slot = used[0]
        used[0] += 1
        return pltpu.make_async_remote_copy(
            src_ref=src, dst_ref=dst, send_sem=send_sem.at[slot], recv_sem=recv_sem.at[slot],
            device_id=at_place(other), device_id_type=MESH,
        )

    def send(src, dst, other):
        copy = remote(src, dst, other)
        copy.start()
        return copy

    half = steps // 2
    away = pl.multiple_of((1 - core) * half, 8)
    near = pl.multiple_of(core * half, 8)

    for load in loads[:3]:
        load.wait()
    trans = trans_ref[...]
    trans_t = trans.T
    scaled_map = map_ref[...] * column(gain_ref[...], gain_ref.shape[1])
    keep = jnp.where(eye(width), 1.0, 0.0) - mm_first(scaled_map, map_ref[...])
    corr_t = mm(trans_t, keep)
    back_t = mm(trans, keep)
    ones = [trans_t, corr_t]
    both = jnp.concatenate(ones, 1)
    twos = mm(jnp.concatenate(ones, 0), both)
    pairs = [twos[a * width:(a + 1) * width, b * width:(b + 1) * width] for a in range(2) for b in range(2)]
    wide = jnp.concatenate(pairs, 1)
    for a in range(4):
        fours = mm(pairs[a], wide)
        for b in range(4):
            table[a * 4 + b] = fours[:, b * width:(b + 1) * width]

    for load in loads[3:]:
        load.wait()
    pl.semaphore_wait(barrier, len(others))
    obs_copy = send(obs_ref.at[0, pl.ds(away, half), :], got_obs, mate(1))
    flags[...] = jnp.broadcast_to(column(flag_ref[...].astype(F32), steps), flags.shape)
    obs_copy.wait_recv()
    own_push = mm_apply(obs_ref[0, pl.ds(near, half), :], scaled_map)
    got_push = mm_apply(got_obs[...], scaled_map)
    push[pl.ds(0, half, stride=2), :] = jnp.where(core == 0, own_push, got_push)
    push[pl.ds(1, half, stride=2), :] = jnp.where(core == 0, got_push, own_push)

    step_flags = [flags[pl.ds(j, chunks, stride=4), :] for j in range(4)]
    step_push = [push[pl.ds(j, chunks, stride=4), :] * step_flags[j] for j in range(4)]

    def advance(state, j, times=mm):
        moved = times(state, both)
        return jnp.where(step_flags[j] > 0, moved[:, width:], moved[:, :width]) + step_push[j]

    state = step_push[0]
    for j in range(1, 4):
        state = advance(state, j, mm_apply)

    def quad(q):
        f = [flag_smem[4 * q + j] for j in range(4)]
        return table[f[0] * 8 + f[1] * 4 + f[2] * 2 + f[3]]

    def spread(row):
        return jnp.broadcast_to(row, (8, width))

    def compose(early, late):
        moved = mm_packed(jnp.concatenate(early, 0), late[0])
        return (moved[:width], moved[width:] + late[1])

    placed = [0]

    def keep_node(mat, vec):
        at = placed[0]
        placed[0] += 1
        held_tree[at, :width] = mat
        held_tree[at, width:] = vec
        return at

    def node(at):
        return (held_tree[at, :width], held_tree[at, width:])

    tree = [[keep_node(quad(q), spread(state[q:q + 1])) for q in range(chunks)]]
    while len(tree[-1]) > 1:
        ids = tree[-1]
        tree.append(
            [keep_node(*compose(node(ids[i]), node(ids[i + 1]))) for i in range(0, len(ids), 2)]
        )
    total = node(tree[-1][0])

    held_powers[0] = back_t
    powers = {1: 0}

    def power(n):
        if n not in powers:
            low = n // 2 if n & (n - 1) == 0 else n & -n
            value = mm(power(low), power(n - low))
            powers[n] = len(powers)
            held_powers[powers[n]] = value
        return held_powers[powers[n]]

    def read_map(ref):
        return (ref[:width], ref[width:])

    def pick(early, late, test):
        return tuple(jnp.where(test, a, b) for a, b in zip(early, late))

    nothing = (jnp.where(eye(width), 1.0, 0.0), jnp.zeros((8, width), F32))
    own_map[:width] = total[0]
    own_map[width:] = total[1]
    copies = [send(own_map, core_map, mate(1))]
    mix_t = mm(trans_t, back_t)
    for n in (1, 2, 3, 4, 8):
        power(n)
    copies[-1].wait_recv()
    other_core = read_map(core_map)
    total = compose(pick(total, other_core, core == 0), pick(other_core, total, core == 0))
    chip = lax.rem(place // 2, 4)
    chip_maps[chip, :width] = total[0]
    chip_maps[chip, width:] = total[1]
    sent = [send(chip_maps.at[chip], chip_maps.at[chip], mate(mask)) for mask in (6, 2, 4)]
    copies += sent
    for n in (12, 16, 32, 48, 64, 128, 256, 512):
        power(n)
    for copy in sent:
        copy.wait_recv()
    maps = [read_map(chip_maps.at[i]) for i in range(4)]
    first_two = compose(maps[0], maps[1])
    all_four = compose(first_two, compose(maps[2], maps[3]))
    onward = remote(next_start, got_start, lax.rem(place + mates, count))

    leap = remote(next_start, got_leap, lax.rem(place + 2 * mates, count))
    lend = remote(own_plane, got_plane, lax.rem(place + mates, count))
    odd = lax.rem(line, 2) == 1
    lends = jnp.logical_and(jnp.logical_not(odd), jnp.logical_and(line > 0, line < lines - 1))
    hands_on = jnp.logical_and(jnp.logical_or(odd, line == 0), line < lines - 1)
    leaps = jnp.logical_and(odd, line < lines - 2)
    borrows = jnp.logical_and(odd, line > 1)

    @pl.when(lends)
    def _():
        own_plane[:width] = all_four[0]
        own_plane[width:] = all_four[1]
        lend.start()

    plane_weights = weights_of(all_four[0])
    origin = spread(init_ref[...])
    beyond = mm_weights(origin, plane_weights) + all_four[1]

    @pl.when(line == 0)
    def _():
        got_start[...] = origin
        next_start[...] = beyond
        onward.start()

    before = pick(compose(first_two, maps[2]), first_two, chip == 3)
    before = pick(maps[0], before, chip == 1)
    before = pick(nothing, before, chip == 0)
    before = pick(compose(before, other_core), before, core == 1)
    for n in list(range(1, mates)) + [mates * n for n in range(1, lines - 1)]:
        power(n * steps)
    across = nothing[0]
    for n in range(1, mates):
        across = jnp.where(mine == mates - 1 - n, power(n * steps), across)
    jumps = [across] + [mm(power(mates * n * steps), across) for n in range(1, lines - 1)]
    for n, jump in enumerate(jumps):
        held_jumps[n * width:(n + 1) * width] = jump
    for n in range(1, mates):
        held_steps[(n - 1) * width:n * width] = power(n * steps)

    before_weights = weights_of(before[0])

    @pl.when(borrows)
    def _():
        lend.wait_recv()
        weights = weights_of(got_plane[:width])
        leap.wait_recv()
        got_start[...] = mm_weights(got_leap[...], weights) + got_plane[width:]

    @pl.when(jnp.logical_and(line > 0, jnp.logical_not(borrows)))
    def _():
        onward.wait_recv()

    start = got_start[...]
    beyond = mm_weights(start, plane_weights) + all_four[1]

    @pl.when(jnp.logical_and(odd, line < lines - 1))
    def _():
        next_start[...] = beyond
        onward.start()

    @pl.when(leaps)
    def _():
        leap.start()

    begin = mm_weights(start, before_weights) + before[1]

    heads = [begin]
    for ids in reversed(tree[:-1]):
        after = []
        for i, head in enumerate(heads):
            mat, vec = node(ids[2 * i])
            after.append(apply_row(head, mat) + vec)
        heads = [x for pair in zip(heads, after) for x in pair]
    lanes = lax.broadcasted_iota(jnp.int32, (8, width), 0)
    tiles = []
    for q in range(0, chunks, 8):
        tile = heads[q]
        for i in range(1, 8):
            tile = jnp.where(lanes == i, heads[q + i], tile)
        tiles.append(tile)
    state = jnp.concatenate(tiles, 0)
    for j in range(4):
        state = advance(state, j, mm_apply)
        push[pl.ds(j, chunks, stride=4), :] = state
    filtered = push[...]

    row_ids = lax.broadcasted_iota(jnp.int32, (steps, width), 0)
    final = jnp.logical_and(row_ids == steps - 1, place == last)
    blended = jnp.where(final, filtered, filtered - mm(filtered, mix_t))

    pad[steps:, :] = jnp.zeros((steps, width), F32)

    def suffixes(rows):
        stride = 1
        while stride < steps:
            pad[:steps, :] = rows
            moved = jnp.concatenate([pad[n * stride:n * stride + steps, :] for n in (1, 2, 3)], 1)
            rows = rows + mm_apply(moved, jnp.concatenate([power(n * stride) for n in (1, 2, 3)], 0))
            stride *= 4
        return rows

    partial = suffixes(blended)
    got_near[mates:] = jnp.zeros((mates, 1, width), F32)
    got_near[mine] = partial[:1]
    sent = [send(got_near.at[mine], got_near.at[mine], mate(mask)) for mask in (6, 7, 2, 3, 4, 5, 1)]
    copies += sent
    steps_halves = halves(held_steps[...])
    for copy in sent:
        copy.wait_recv()
    rows = [got_near[n] for n in range(mates)]
    after = [got_near[mine + 1 + n] for n in range(mates)]
    both_rows = jnp.concatenate(
        [jnp.concatenate([spread(a), spread(b)], 0) for a, b in zip(rows[1:], after[1:])], 1
    )
    folded = mm_halves(both_rows, steps_halves)
    got_far[lines - 1] = folded[:1] + rows[0]
    tail = folded[8:] + spread(after[0])
    sent = [
        send(got_far.at[lines - 1], got_far.at[n], lax.rem(place + mates * (2 * lines - 1 - n), count))
        for n in range(lines - 1)
    ]
    copies += sent
    jumps_halves = halves(held_jumps[...])
    for copy in sent:
        copy.wait_recv()
    later = [
        jnp.where(n < lines - 1 - line, spread(got_far[n]), 0.0) for n in range(lines - 1)
    ]
    arriving = tail + mm_halves(jnp.concatenate(later, 1), jumps_halves)
    entry = jnp.where(row_ids == steps - 1, mm(arriving, back_t)[:1], 0.0)
    smoothed = partial + suffixes(entry)
    smooth_ref[...] = smoothed

    pad[:steps, :] = smoothed
    pad[steps:steps + 8, :] = arriving
    following = pad[1:steps + 1, :]
    counted = jnp.where(final, 0.0, smoothed)
    moments = mm_apply(counted.T, jnp.concatenate([smoothed, following], 1))
    owned = width // mates
    for n in range(mates):
        moment[n] = moments[n * owned:(n + 1) * owned]
    sent = [
        send(moment.at[lax.rem(mate(mask), mates)], got_moment.at[mask], mate(mask))
        for mask in (6, 7, 2, 3, 4, 5, 1)
    ]
    copies += sent
    pair_count = F32(steps * (last + 1) - 1)
    lag_t = pair_count * lax.dot_general(
        back_t, cov_ref[...], (((0,), (1,)), ((), ())),
        precision=lax.Precision.HIGHEST, preferred_element_type=F32,
    )
    for copy in sent:
        copy.wait_recv()
    held = moment[mine]
    for n in range(1, mates):
        held = held + got_moment[n]
    line_moment[line] = held
    sent = [
        send(line_moment.at[line], line_moment.at[line], lax.rem(place + mates * n, count))
        for n in range(1, lines)
    ]
    copies += sent
    for copy in sent:
        copy.wait_recv()
    held = line_moment[0]
    for n in range(1, lines):
        held = held + line_moment[n]
    full_moment[mine] = held
    sent = [
        send(full_moment.at[mine], full_moment.at[mine], mate(mask)) for mask in (6, 7, 2, 3, 4, 5, 1)
    ]
    copies += sent
    for copy in sent:
        copy.wait_recv()
    extra = jnp.concatenate([pair_count * cov_ref[...], lag_t], 1)
    for n in range(mates):
        rows = slice(n * owned, (n + 1) * owned)
        sums_ref[rows, :] = full_moment[n] + extra[rows]

    @pl.when(hands_on)
    def _():
        onward.wait_send()

    @pl.when(leaps)
    def _():
        leap.wait_send()

    @pl.when(lends)
    def _():
        lend.wait_send()

    obs_copy.wait_send()
    for copy in copies:
        copy.wait_send()


def product(x, y):
    return [
        [sum((x[i][k] * y[k][j] for k in range(1, len(y))), x[i][0] * y[0][j]) for j in range(len(y[0]))]
        for i in range(len(x))
    ]


def small_inverse(d):
    n = len(d)
    if n == 1:
        return [[1.0 / d[0][0]]]
    if n == 2:
        det = 1.0 / (d[0][0] * d[1][1] - d[0][1] * d[0][1])
        off = -d[0][1] * det
        return [[d[1][1] * det, off], [off, d[0][0] * det]]
    h = n // 2
    head = small_inverse([r[:h] for r in d[:h]])
    side = [r[h:] for r in d[:h]]
    spread = product(head, side)
    fill = product([list(x) for x in zip(*side)], spread)
    rest = small_inverse([[d[h + i][h + j] - fill[i][j] for j in range(h)] for i in range(h)])
    back = product(spread, rest)
    fill = product(back, [list(x) for x in zip(*spread)])
    top = [[head[i][j] + fill[i][j] for j in range(h)] + [-x for x in back[i]] for i in range(h)]
    return top + [[-back[j][i] for j in range(h)] + rest[i] for i in range(h)]


def combine(rows, weights):
    total = rows[0] * weights[0]
    for row, weight in zip(rows[1:], weights[1:]):
        total = total + row * weight
    return total


def solve_kernel(sums_ref, smooth_ref, out_ref, smooth_out_ref):
    smooth_out_ref[...] = smooth_ref[...]
    width = out_ref.shape[0]
    groups = width // 8
    per = 4
    full = (8, width)
    left = [sums_ref[8 * g:8 * g + 8, :width] for g in range(groups)]
    right = [sums_ref[8 * g:8 * g + 8, width:] for g in range(groups)]
    lane = lax.broadcasted_iota(jnp.int32, (1, width), 1)
    sub = lax.broadcasted_iota(jnp.int32, full, 0)

    def spread_row(tile, i):
        return jnp.broadcast_to(tile[i:i + 1, :], full)

    for at in range(0, groups, per):
        panel = range(at, at + per)
        for pivot in panel:
            cols = {
                g: [jnp.broadcast_to(left[g][:, k:k + 1], full) for k in range(8 * pivot, 8 * pivot + 8)]
                for g in panel
            }
            inverse = small_inverse(
                [[spread_row(cols[pivot][max(i, j)], min(i, j)) for j in range(8)] for i in range(8)]
            )
            for side in (left, right):
                rows = [spread_row(side[pivot], j) for j in range(8)]
                solved = [combine(rows, inverse[i]) for i in range(8)]
                for g in panel:
                    if g == pivot:
                        tile = solved[0]
                        for j in range(1, 8):
                            tile = jnp.where(sub == j, solved[j], tile)
                        side[g] = tile
                    else:
                        side[g] = side[g] - combine(cols[g], solved)
        mask = jnp.logical_and(lane >= 8 * at, lane < 8 * (at + per))
        order = [g % groups for g in range(at + per, at + groups)]
        rows = [jnp.concatenate([left[g], right[g]], 1) for g in panel]
        before, after = 8 * at, 8 * (groups - at - per)
        if before:
            rows = [jnp.zeros((before, 2 * width), F32)] + rows
        if after:
            rows = rows + [jnp.zeros((after, 2 * width), F32)]
        change = mm(
            jnp.concatenate([jnp.where(mask, left[g], 0.0) for g in order], 0), jnp.concatenate(rows, 0)
        )
        for i, g in enumerate(order):
            left[g] = left[g] - change[8 * i:8 * i + 8, :width]
            right[g] = right[g] - change[8 * i:8 * i + 8, width:]
    out_ref[...] = jnp.concatenate(right, 0).T


def local(levels, obs_store, observed, transition, obs_map, gain_weights, init_mean, smoothed_cov):
    steps = observed.shape[0]
    width = transition.shape[0]
    vmem = pl.BlockSpec(memory_space=pltpu.VMEM)
    count = 2**levels
    mates = 8
    lines = count // mates
    copies = 8 + 3 * (mates - 1) + 2 * (lines - 1)
    chip_map = (width + 8, width)
    owned = (width // mates, 2 * width)
    smoothed, sums = pl.pallas_call(
        functools.partial(em_kernel, levels),
        out_shape=(
            jax.ShapeDtypeStruct((steps, width), F32),
            jax.ShapeDtypeStruct((width, 2 * width), F32),
        ),
        in_specs=[pl.BlockSpec(memory_space=pltpu.HBM)] * 8,
        out_specs=(vmem, vmem),
        scratch_shapes=[
            pltpu.VMEM(obs_store.shape, F32),
            pltpu.SMEM((steps,), jnp.int32),
            pltpu.VMEM((1, steps), jnp.int32),
            pltpu.VMEM((width, width), F32),
            pltpu.VMEM(obs_map.shape, F32),
            pltpu.VMEM((1, obs_map.shape[0]), F32),
            pltpu.VMEM((1, width), F32),
            pltpu.VMEM((width, width), F32),
            pltpu.SemaphoreType.DMA((8,)),
            pltpu.VMEM((steps // 2, obs_map.shape[0]), F32),
            pltpu.VMEM((16, width, width), F32),
            pltpu.VMEM((steps, width), F32),
            pltpu.VMEM((steps, width), F32),
            pltpu.VMEM((2 * steps, width), F32),
            pltpu.VMEM(chip_map, F32),
            pltpu.VMEM(chip_map, F32),
            pltpu.VMEM((4, *chip_map), F32),
            pltpu.VMEM((8, width), F32),
            pltpu.VMEM((8, width), F32),
            pltpu.VMEM((8, width), F32),
            pltpu.VMEM(chip_map, F32),
            pltpu.VMEM(chip_map, F32),
            pltpu.VMEM((2 * mates, 1, width), F32),
            pltpu.VMEM((lines, 1, width), F32),
            pltpu.VMEM(((mates - 1) * width, width), F32),
            pltpu.VMEM(((lines - 1) * width, width), F32),
            pltpu.VMEM((mates, *owned), F32),
            pltpu.VMEM((mates, *owned), F32),
            pltpu.VMEM((lines, *owned), F32),
            pltpu.VMEM((mates, *owned), F32),
            pltpu.VMEM((steps // 2 - 1, width + 8, width), F32),
            pltpu.VMEM((24 + lines, width, width), F32),
            pltpu.SemaphoreType.DMA((copies,)),
            pltpu.SemaphoreType.DMA((copies,)),
        ],
        compiler_params=pltpu.CompilerParams(
            collective_id=0, has_side_effects=True, vmem_limit_bytes=24 * 2**20
        ),
    )(*[
        pltpu.with_memory_space_constraint(x, pltpu.HBM)
        for x in (
            obs_store, observed, observed.reshape(1, -1), transition, obs_map,
            gain_weights.reshape(1, -1), init_mean.reshape(1, -1), smoothed_cov,
        )
    ])
    new_transition, smoothed = pl.pallas_call(
        solve_kernel,
        out_shape=(
            jax.ShapeDtypeStruct((width, width), F32),
            jax.ShapeDtypeStruct((steps, width), F32),
        ),
        in_specs=[vmem, vmem],
        out_specs=(vmem, vmem),
        compiler_params=pltpu.CompilerParams(vmem_limit_bytes=24 * 2**20),
    )(sums, smoothed)
    return (smoothed, new_transition)


def solution(mesh):
    levels = (mesh.shape["tm"] * mesh.shape["replay"]).bit_length() - 1
    return jax.shard_map(
        functools.partial(local, levels),
        mesh=mesh,
        in_specs=(P("replay", "tm", None), P(("tm", "replay")), P(), P(), P(), P(), P()),
        out_specs=(P(("tm", "replay"), None), P()),
        check_vma=False,
    )
```
